512 devices in a mesh: dp: 16 (over y, core), seq: 32 (over z, x).
Axes of the slice: x: 4, y: 8, z: 8, core: 2. Of those that a mesh axis runs over, the one named last changes fastest.
Arguments:
- hidden: bfloat16 [65536, 2048], P(('dp', 'seq')), may hold values from -6 to 6
- queries: bfloat16 [65536, 2048], P(('dp', 'seq')), may hold values from -360 to 360
- values: bfloat16 [65536, 512], P(('dp', 'seq')), may hold values from -6 to 6
- row_target: int32 [65536], P(('dp', 'seq')), may hold values from 0 to 4095, as said below
- key_weight: bfloat16 [2048, 512], P(('dp', 'seq')), may hold values from -0.125 to 0.125
- dialogue_lengths: int32 [16, 64], P('dp'), may hold values from 1 to 256, 4096 in all within a row
- teacher_pick: int32 [65536, 128], P(('dp', 'seq')), may hold values from 0 to 65279
- teacher_prob: float32 [65536, 128], P(('dp', 'seq')), may hold values from 0.02 to 1
Outputs:
- attn_out: bfloat16 [65536, 2048], P(('dp', 'seq'))
- token_loss: float32 [65536], P(('dp', 'seq'))
- weight_grad: float32 [2048, 512], P(('dp', 'seq'))
The draws below stay inside these ranges and needn't reach their ends.
Inputs may be any that keep to these rules, and one draw needn't show every extreme that they name: Within each pack, row_target holds every position 0 to 4095 once. Of the 128 rows of one device, at most 6 have targets in one block of 128 positions (target // 128 names the block), and in every draw some device sends exactly 6 to some block.
All inputs are finite; a program needn't handle non-finite values.
Results may differ from the reference program's by a relative error of at most 0.012.
The reference program's roundings to bfloat16 on the way count: a program that leaves them out, or rounds other values in their place, can miss the bound.
Values may be sent and summed in bfloat16 or wider, within the bound.
No kernel may reach another device: no remote copies, remote signals or barrier semaphores. Data moves between devices by JAX's collectives and lax.ppermute only.
A program may use at most 64 MiB of HBM per device.

```python
import math
import jax
import jax.numpy as jnp
import numpy as np
from jax import lax

D = 2048
HEADS = 16
KV_HEADS = 4
HEAD_DIM = 128
TOPK = 8
SPAN = 2
TOK_DEV = 128
PACK = 4096
TOKENS = 65536
MOST = 256
NDIAL = 64
N_DP = 16
N_SEQ = 32


def shuffle_entries(entries, shuffle_key):
    return entries[jax.random.permutation(shuffle_key, entries.shape[0])]


def pack_targets(pack_key):
    per_shard = TOK_DEV // N_SEQ
    halfway = per_shard // 2
    pair_count = N_SEQ // 2
    sub_keys = jax.random.split(pack_key, 5)
    moves = jax.random.randint(sub_keys[0], (pair_count,), -halfway, halfway + 1)
    moves = moves.at[0].set(halfway)
    shares = jnp.concatenate([per_shard + moves, per_shard - moves]).astype(jnp.int32)
    shares = shares[jax.random.permutation(sub_keys[1], N_SEQ)]
    left_order = jax.random.permutation(sub_keys[2], N_SEQ)
    right_order = jax.random.permutation(sub_keys[3], N_SEQ)
    counts = shares[(right_order[None, :] - left_order[:, None]) % N_SEQ]
    earlier = (jnp.cumsum(counts, axis=0) - counts).astype(jnp.int32)
    upto = jnp.cumsum(counts, axis=1).astype(jnp.int32)
    lower = upto - counts
    ordinal = jnp.arange(TOK_DEV, dtype=jnp.int32)
    shard_of = jnp.sum((upto[:, None, :] <= ordinal[None, :, None]).astype(jnp.int32), axis=2)
    within = ordinal[None, :] - jnp.take_along_axis(lower, shard_of, axis=1)
    target = shard_of * TOK_DEV + jnp.take_along_axis(earlier, shard_of, axis=1) + within
    mix_keys = jax.random.split(sub_keys[4], N_SEQ)
    target = jax.vmap(shuffle_entries)(target, mix_keys)
    return target.reshape(PACK).astype(jnp.int32)


def draw_row_target(key, part):
    pack_keys = jax.random.split(jax.random.fold_in(key, 11), TOKENS // PACK)
    return jax.vmap(pack_targets)(pack_keys).reshape(TOKENS)


def draw_queries(key, part):
    first_key = jax.random.fold_in(jax.random.fold_in(key, 23), 0)
    normal_part = jnp.clip(jax.random.normal(first_key, (TOKENS, HEADS * HEAD_DIM), jnp.float32), -6.0, 6.0)
    return normal_part.astype(jnp.bfloat16)


def with_ends(values, stream_key, smallest, largest):
    longest = values.shape.index(max(values.shape))
    spots = []
    for shift in (0, 1):
        where = [jax.random.randint(jax.random.fold_in(stream_key, axis), (), 0, length) for axis, length in enumerate(values.shape)]
        where[longest] = (where[longest] + shift) % values.shape[longest]
        spots.append(tuple(where))
    return values.at[spots[0]].set(smallest).at[spots[1]].set(largest)


def shard_levels(own_key, shape, shards, low, top_value):
    def one(position, parts):
        heights = jax.random.uniform(jax.random.fold_in(jax.random.fold_in(own_key, 6), position), (parts,), jnp.float32, low / len(shards), top_value / len(shards))
        return jnp.repeat(jnp.exp(heights), shape[position] // parts).reshape((-1,) + (1,) * (len(shape) - position - 1))

    gain = one(*shards[0])
    for cut in shards[1:]:
        gain = gain * one(*cut)
    return gain


def split_up(count, total, bound, skew):
    portions = [(1 << 20) // math.isqrt(standing ** skew) + 1 for standing in range(2, count + 1)]
    spare, given = total - bound - (count - 1), [1] * (count - 1)
    while spare > 0:
        movable = [i for i in range(count - 1) if given[i] < bound]
        pool, budget = sum([portions[i] for i in movable]), spare
        for i in movable:
            addition = min(bound - given[i], max(1, budget * portions[i] // pool), spare)
            given[i] = given[i] + addition
            spare = spare - addition
    return np.array([bound] + given)


def ragged_sizes(rng, amount, total, limit, lean):
    if amount == 2:
        one = jax.random.randint(rng, (), max(1, total - limit), min(limit, total - 1) + 1)
        return jnp.stack([one, total - one])
    sizes = jnp.asarray(split_up(amount, total, limit, lean), jnp.int32)
    couples = (amount - 1) // 2
    donor, taker = sizes[1:1 + 2 * couples:2], sizes[2:2 + 2 * couples:2]
    margin = jnp.minimum(donor - 1, limit - taker)
    moved = jax.random.randint(jax.random.fold_in(rng, 1), (couples,), 0, 1 << 20) % (margin + 1)
    sizes = sizes.at[1:1 + 2 * couples:2].set(donor - moved).at[2:2 + 2 * couples:2].set(taker + moved)
    return sizes[jax.random.permutation(jax.random.fold_in(rng, 2), amount)]


def gaussian(stream_key, extent, scale, limit, cuts=(), kind=jnp.bfloat16):
    values = jax.random.normal(stream_key, extent, jnp.float32) * scale
    if len(cuts) > 0:
        values = shard_levels(stream_key, extent, cuts, -0.22, 0.18) * values
    return jnp.clip(values, min=-limit, max=limit).astype(kind)


def setup_inputs(seed: int = 0) -> dict:
    seeds = jax.random.split(jax.random.key(seed), 9)
    hidden = gaussian(seeds[0], (TOKENS, D), 1.0, 6.0, ((0, 512),))
    queries = draw_queries(jax.random.fold_in(seeds[8], 71), 0)
    values = gaussian(seeds[2], (TOKENS, KV_HEADS * HEAD_DIM), 1.0, 6.0, ((0, 512),))
    row_target = draw_row_target(jax.random.fold_in(seeds[8], 71), 0)
    key_weight = gaussian(seeds[4], (D, KV_HEADS * HEAD_DIM), D ** -0.5, 0.125, ((0, 512),))
    dialogue_lengths = jax.vmap(lambda own: ragged_sizes(own, NDIAL, PACK, MOST, 2))(jax.random.split(seeds[5], N_DP)).reshape((N_DP, NDIAL)).astype(jnp.int32)
    teacher_pick = with_ends(jax.random.randint(seeds[6], (TOKENS, HEADS * TOPK), 0, 65280), jax.random.fold_in(seeds[6], 1), 0, 65279).astype(jnp.int32)
    teacher_prob = jnp.clip(jnp.exp(math.log(1.0) - 3.912023 * jax.random.uniform(seeds[7], (TOKENS, HEADS * TOPK), jnp.float32) ** shard_levels(seeds[7], (TOKENS, HEADS * TOPK), ((0, 512),), -0.2, 0.2)), 0.02, 1.0)
    return dict(hidden=hidden, queries=queries, values=values, row_target=row_target, key_weight=key_weight, dialogue_lengths=dialogue_lengths, teacher_pick=teacher_pick, teacher_prob=teacher_prob)


negative = -1.0e30
rope_base = 500000.0


def rotate(matrix, positions, direction):
    count = matrix.shape[0]
    split = matrix.reshape(count, -1, HEAD_DIM)
    halfway = HEAD_DIM // 2
    frequency = rope_base ** (-2.0 * jnp.arange(halfway, dtype=jnp.float32) / HEAD_DIM)
    angle = positions.astype(jnp.float32)[:, None] * frequency[None, :]
    cosine = jnp.cos(angle)[:, None, :]
    sine = direction * jnp.sin(angle)[:, None, :]
    first_half = split[..., :halfway]
    second_half = split[..., halfway:]
    joined = jnp.concatenate([first_half * cosine - second_half * sine, second_half * cosine + first_half * sine], axis=-1)
    return joined.reshape(count, -1)


def dialogue_starts(lengths, positions):
    ending = jnp.cumsum(lengths).astype(jnp.int32)
    picked = jnp.where(ending[None, :] <= positions[:, None], lengths[None, :], 0)
    return jnp.sum(picked, axis=1).astype(jnp.int32)


def block_targets(label_index, label_prob, key_start, width, head_count):
    row_count = label_index.shape[0]
    within = label_index - key_start
    within = jnp.where((within >= 0) & (within < width), within, width).astype(jnp.int32)
    head_ids = jnp.broadcast_to(jnp.arange(head_count, dtype=jnp.int32)[None, :, None], label_index.shape)
    row_ids = jnp.broadcast_to(jnp.arange(row_count, dtype=jnp.int32)[:, None, None], label_index.shape)
    table = jnp.zeros((head_count, row_count, width), jnp.float32)
    return table.at[head_ids, row_ids, within].add(label_prob, mode="drop")


def reference(hidden, queries, values, row_target, key_weight, dialogue_lengths, teacher_pick, teacher_prob):
    pack_count = TOKENS // PACK
    group_size = HEADS // KV_HEADS
    kv_width = KV_HEADS * HEAD_DIM
    padding = SPAN * TOK_DEV
    window = padding + TOK_DEV
    scaling = HEAD_DIM ** -0.5

    def one_pack(item):
        hidden_in, queries_in, values_in, target_in, lengths, pick_in, prob_in = item
        hidden_seq = jnp.zeros((PACK, D), jnp.bfloat16).at[target_in].set(hidden_in)
        queries_seq = jnp.zeros((PACK, HEADS * HEAD_DIM), jnp.bfloat16).at[target_in].set(queries_in)
        values_seq = jnp.zeros((PACK, kv_width), jnp.bfloat16).at[target_in].set(values_in)
        positions = jnp.arange(PACK, dtype=jnp.int32)
        starts = dialogue_starts(lengths, positions)
        projected = jnp.dot(hidden_seq, key_weight, preferred_element_type=jnp.float32)
        keys_seq = rotate(projected, positions, 1.0).astype(jnp.bfloat16)
        keys_pad = jnp.concatenate([jnp.zeros((padding, kv_width), jnp.bfloat16), keys_seq], axis=0)
        values_pad = jnp.concatenate([jnp.zeros((padding, kv_width), jnp.bfloat16), values_seq], axis=0)

        def block(carry, number):
            first_row = (number * TOK_DEV).astype(jnp.int32)
            query_pos = first_row + jnp.arange(TOK_DEV, dtype=jnp.int32)
            query_block = lax.dynamic_slice_in_dim(queries_seq, first_row, TOK_DEV, 0)
            query_start = lax.dynamic_slice_in_dim(starts, first_row, TOK_DEV, 0)
            key_block = lax.dynamic_slice_in_dim(keys_pad, first_row, window, 0)
            value_block = lax.dynamic_slice_in_dim(values_pad, first_row, window, 0)
            key_pos = first_row - padding + jnp.arange(window, dtype=jnp.int32)
            pick_block = lax.dynamic_slice_in_dim(pick_in, first_row, TOK_DEV, 0)
            prob_block = lax.dynamic_slice_in_dim(prob_in, first_row, TOK_DEV, 0).reshape(TOK_DEV, HEADS, TOPK)
            reach = (query_pos - query_start + 1)[:, None]
            label_index = (query_start[:, None] + pick_block % reach).reshape(TOK_DEV, HEADS, TOPK).astype(jnp.int32)
            query_heads = query_block.reshape(TOK_DEV, KV_HEADS, group_size, HEAD_DIM).astype(jnp.float32)
            key_heads = key_block.reshape(window, KV_HEADS, HEAD_DIM).astype(jnp.float32)
            value_heads = value_block.reshape(window, KV_HEADS, HEAD_DIM).astype(jnp.float32)
            score = jnp.einsum("tkgd,wkd->kgtw", query_heads, key_heads) * scaling
            allowed = (key_pos[None, :] >= query_start[:, None]) & (key_pos[None, :] <= query_pos[:, None])
            held = jnp.where(allowed[None, None], score, negative)
            top_score = jnp.max(held, axis=-1)
            lse = top_score + jnp.log(jnp.sum(jnp.exp(held - top_score[..., None]), axis=-1))
            weight = jnp.exp(held - lse[..., None])
            table = block_targets(label_index, prob_block, first_row - padding, window, HEADS)
            table = table.reshape(KV_HEADS, group_size, TOK_DEV, window)
            mass = jnp.sum(prob_block, axis=2).T.reshape(KV_HEADS, group_size, TOK_DEV)
            entropy = jnp.sum(prob_block * jnp.log(prob_block), axis=(1, 2))
            picked = jnp.sum(table * score, axis=(0, 1, 3))
            loss = (entropy - picked + jnp.sum(mass * lse, axis=(0, 1))) / HEADS
            rounded = weight.astype(jnp.bfloat16).astype(jnp.float32)
            output = jnp.einsum("kgtw,wkd->tkgd", rounded, value_heads).astype(jnp.bfloat16)
            output = output.reshape(TOK_DEV, HEADS * HEAD_DIM)
            slope = ((weight * mass[..., None] - table) / HEADS).astype(jnp.bfloat16).astype(jnp.float32)
            gradient = jnp.einsum("kgtw,tkgd->wkd", slope, query_heads) * scaling
            gradient = gradient.reshape(window, kv_width)
            current = lax.dynamic_slice_in_dim(carry, first_row, window, 0)
            carry = lax.dynamic_update_slice_in_dim(carry, current + gradient, first_row, 0)
            return carry, (output, loss)

        initial = jnp.zeros((PACK + padding, kv_width), jnp.float32)
        grads_pad, (outputs, losses) = lax.scan(block, initial, jnp.arange(N_SEQ, dtype=jnp.int32))
        key_grad = rotate(grads_pad[padding:], positions, -1.0).astype(jnp.bfloat16)
        term = jnp.dot(hidden_seq.T, key_grad, preferred_element_type=jnp.float32)
        return outputs.reshape(PACK, HEADS * HEAD_DIM), losses.reshape(PACK), term

    items = (
        hidden.reshape(pack_count, PACK, D),
        queries.reshape(pack_count, PACK, HEADS * HEAD_DIM),
        values.reshape(pack_count, PACK, kv_width),
        row_target.reshape(pack_count, PACK),
        dialogue_lengths,
        teacher_pick.reshape(pack_count, PACK, HEADS * TOPK),
        teacher_prob.reshape(pack_count, PACK, HEADS * TOPK),
    )
    outputs, losses, terms = lax.map(one_pack, items)
    weight_grad = jnp.sum(terms, axis=0) * (TOKENS ** -0.5)
    return outputs.reshape(TOKENS, HEADS * HEAD_DIM), losses.reshape(TOKENS), weight_grad
```

```python
import jax
import jax.numpy as jnp
import numpy as np
from jax import lax
from jax.sharding import Mesh
from jax.sharding import PartitionSpec as P

HEAD_DIM = 128
SPAN = 2
SLOTS = 6

negative = -1e30
rope_base = 500000.0

SEQ = ("z", "xh", "xl")
EVERY = ("y", "core") + SEQ


def exchange(pieces, axes):
    return lax.all_to_all(pieces, axes, split_axis=0, concat_axis=0, tiled=True)


def seq_shift(shard, by):
    devices = lax.axis_size(SEQ)
    pairs = [(i, i + by) for i in range(devices) if 0 <= i + by < devices]
    return lax.ppermute(shard, SEQ, pairs)


def core_swap(shard):
    return lax.ppermute(shard, "core", [(0, 1), (1, 0)])


def turn_angles(positions):
    halfway = HEAD_DIM // 2
    frequency = rope_base ** (-2.0 * jnp.arange(halfway, dtype=jnp.float32) / HEAD_DIM)
    angle = positions.astype(jnp.float32)[:, None] * frequency[None, :]
    return jnp.cos(angle)[:, None, :], jnp.sin(angle)[:, None, :]


def rotate(matrix, cosine, sine):
    count = matrix.shape[0]
    halfway = HEAD_DIM // 2
    split = matrix.reshape(count, -1, HEAD_DIM)
    first_half = split[..., :halfway]
    second_half = split[..., halfway:]
    joined = jnp.concatenate(
        [first_half * cosine - second_half * sine, second_half * cosine + first_half * sine],
        axis=-1,
    )
    return joined.reshape(count, -1)


def dialogue_starts(lengths, positions):
    ending = jnp.cumsum(lengths)
    picked = jnp.where(ending[None, :] <= positions[:, None], lengths[None, :], 0)
    return jnp.sum(picked, axis=1)


def block_targets(label_index, label_prob, key_start, width):
    within = label_index - key_start
    columns = jnp.arange(width, dtype=jnp.int32)
    matches = within[..., None] == columns[None, None, None, :]
    table = jnp.sum(jnp.where(matches, label_prob[..., None], 0.0), axis=2)
    return jnp.transpose(table, (1, 0, 2))


def weight_pieces(key_weight):
    rows, columns = key_weight.shape
    lines = lax.axis_size("y")
    got = exchange(jnp.broadcast_to(key_weight, (2 * lines, rows, columns)), ("y", "xl"))
    tiles = got.reshape(lines, 2 * rows, columns)
    half = lines // 2
    mine = lax.dynamic_slice_in_dim(tiles, lax.axis_index("xl") * half, half, 0)
    return jnp.transpose(mine, (1, 0, 2)).reshape(2 * rows, half * columns)


def local(
    hidden, queries, values, row_target, key_weight, dialogue_lengths, teacher_pick, teacher_prob
):
    bf16, f32 = jnp.bfloat16, jnp.float32
    local_rows, width = hidden.shape
    seq_count = lax.axis_size(SEQ)
    seq_index = lax.axis_index(SEQ)
    lines = lax.axis_size("y")
    device_count = seq_count * lines * lax.axis_size("core")
    head_count = queries.shape[1] // HEAD_DIM
    kv_width = values.shape[1]
    kv_count = kv_width // HEAD_DIM
    group_size = head_count // kv_count
    top_count = teacher_pick.shape[1] // head_count
    scaling = HEAD_DIM ** (-0.5)

    destination = row_target // local_rows
    offset_in = row_target - destination * local_rows
    order = jnp.arange(local_rows, dtype=jnp.int32)
    earlier = (destination[None, :] == destination[:, None]) & (order[None, :] < order[:, None])
    rank_in = jnp.sum(earlier.astype(jnp.int32), axis=1)
    tiles = (2 * width + kv_width) // HEAD_DIM
    extra = tiles // 4
    main = tiles - extra
    rows_all = jnp.concatenate([hidden, queries, values], axis=1)
    parcel_row = jnp.arange(seq_count * 8, dtype=jnp.int32)
    block_of, place = parcel_row // 8, parcel_row % 8
    to_block = destination[None, :] == block_of[:, None]
    low = to_block & (place[:, None] == rank_in[None, :]) & (place[:, None] < SLOTS)
    packed = []
    metas = []
    for m in range(3):
        high = to_block & (place[:, None] - SLOTS + 2 * m == rank_in[None, :]) & (place[:, None] >= SLOTS)
        select = jnp.concatenate([low, high], axis=1).astype(bf16)
        left = rows_all[:, : main * HEAD_DIM].reshape(local_rows, main // 3, 3, HEAD_DIM)[:, :, m]
        left = left.reshape(local_rows, main // 3 * HEAD_DIM)
        both = jnp.concatenate([left, rows_all[:, main * HEAD_DIM :]], axis=0)
        packed.append(jnp.dot(select, both, preferred_element_type=f32).astype(bf16))
        shifted = (offset_in - local_rows).astype(f32)
        meta = jnp.sum(jnp.where(low | high, shifted[None, :], 0.0), axis=1) + local_rows
        metas.append(meta)
    body = jnp.stack([p.reshape(-1, main // 3, HEAD_DIM) for p in packed], axis=2).reshape(
        -1, main * HEAD_DIM
    )
    lane = jnp.arange(HEAD_DIM, dtype=jnp.int32)[None, :]
    meta_tile = jnp.where(
        lane == 0, metas[0][:, None], jnp.where(lane == 1, metas[1][:, None], metas[2][:, None])
    ).astype(bf16)
    passed_on = weight_pieces(key_weight)
    payload = jnp.concatenate(
        [
            jnp.concatenate([body, meta_tile], axis=1).reshape(seq_count, 8, -1),
            jnp.broadcast_to(passed_on[None], (seq_count,) + passed_on.shape),
        ],
        axis=2,
    )
    received = exchange(payload, SEQ)

    flat = received.reshape(seq_count * 8, -1)
    meta_got = flat[:, main * HEAD_DIM : main * HEAD_DIM + 3].astype(f32)
    token = jnp.arange(local_rows, dtype=f32)
    is_low = place < SLOTS
    mains, extras = [], 0.0
    for m in range(3):
        hit = meta_got[:, m][None, :] == token[:, None]
        select = jnp.concatenate([hit & is_low[None, :], hit & ~is_low[None, :]], axis=0).astype(bf16)
        part = flat[:, : main * HEAD_DIM].reshape(-1, main // 3, 3, HEAD_DIM)[:, :, m]
        part = part.reshape(seq_count * 8, -1)
        done = jnp.dot(select, part, preferred_element_type=f32)
        mains.append(done[:local_rows].astype(bf16).reshape(local_rows, main // 3, HEAD_DIM))
        extras = extras + done[local_rows:]
    rows_seq = jnp.concatenate(
        [jnp.stack(mains, axis=2).reshape(local_rows, -1), extras.astype(bf16)], axis=1
    )
    hidden_seq = rows_seq[:, :width]
    queries_seq = rows_seq[:, width : 2 * width]
    values_seq = rows_seq[:, 2 * width :]

    half = lines // 2
    weight_got = received[:, :, (main + 1) * HEAD_DIM :].reshape(
        seq_count // 2, 2, 8, half, kv_width
    )
    own_half = jnp.transpose(weight_got, (1, 3, 0, 2, 4)).reshape(lines, local_rows, kv_width)
    other_half = core_swap(own_half)
    core = lax.axis_index("core")
    first = jnp.where(core == 0, own_half, other_half)
    second = jnp.where(core == 0, other_half, own_half)
    weight = jnp.stack([first, second], axis=1).reshape(width, kv_width)

    positions = seq_index * local_rows + jnp.arange(local_rows, dtype=jnp.int32)
    cosine, sine = turn_angles(positions)
    keys_seq = rotate(
        jnp.dot(hidden_seq, weight, preferred_element_type=f32), cosine, sine
    ).astype(bf16)
    starts = dialogue_starts(dialogue_lengths[0], positions)
    reach = (positions - starts + 1)[:, None]
    label_index = (starts[:, None] + teacher_pick % reach).reshape(
        local_rows, head_count, top_count
    )
    label_prob = teacher_prob.reshape(local_rows, head_count, top_count)
    target_mass = jnp.sum(label_prob, axis=2).T.reshape(kv_count, group_size, local_rows)
    entropy = jnp.sum(label_prob * jnp.log(label_prob), axis=(1, 2))
    query_heads = queries_seq.reshape(local_rows, kv_count, group_size, HEAD_DIM)
    blocks = [(keys_seq, values_seq)]
    for distance in range(1, SPAN + 1):
        blocks.append((seq_shift(keys_seq, distance), seq_shift(values_seq, distance)))

    def scores_of(key_block, key_start):
        key_heads = key_block.reshape(local_rows, kv_count, HEAD_DIM)
        score = (
            jnp.einsum("tkgd,wkd->kgtw", query_heads, key_heads, preferred_element_type=f32)
            * scaling
        )
        key_pos = key_start + jnp.arange(local_rows, dtype=jnp.int32)
        allowed = (key_pos[None, :] >= starts[:, None]) & (key_pos[None, :] <= positions[:, None])
        held = jnp.where(allowed[None, None], score, negative)
        table = block_targets(label_index, label_prob, key_start, local_rows)
        return (score, held, table.reshape(kv_count, group_size, local_rows, local_rows))

    tops, totals, pickings = ([], [], [])
    for distance, (key_block, value_block) in enumerate(blocks):
        key_start = (seq_index - distance) * local_rows
        score, held, table = scores_of(key_block, key_start)
        block_top = jnp.max(held, axis=-1)
        tops.append(block_top)
        totals.append(jnp.sum(jnp.exp(held - block_top[..., None]), axis=-1))
        pickings.append(jnp.sum(table * score, axis=-1))
    top_all = jnp.max(jnp.stack(tops), axis=0)
    total_all = jnp.sum(jnp.stack(totals) * jnp.exp(jnp.stack(tops) - top_all[None]), axis=0)
    lse = top_all + jnp.log(total_all)
    picked_all = jnp.sum(jnp.stack(pickings), axis=0)
    token_loss = (
        entropy - jnp.sum(picked_all, axis=(0, 1)) + jnp.sum(target_mass * lse, axis=(0, 1))
    ) / head_count

    output_sum = jnp.zeros((local_rows, kv_count, group_size, HEAD_DIM), f32)
    block_grads = []
    for distance, (key_block, value_block) in enumerate(blocks):
        key_start = (seq_index - distance) * local_rows
        score, held, table = scores_of(key_block, key_start)
        weight_of = jnp.exp(held - lse[..., None])
        value_heads = value_block.reshape(local_rows, kv_count, HEAD_DIM)
        output_sum = output_sum + jnp.einsum(
            "kgtw,wkd->tkgd", weight_of.astype(bf16), value_heads, preferred_element_type=f32
        )
        slope = ((weight_of * target_mass[..., None] - table) / head_count).astype(bf16)
        gradient = (
            jnp.einsum("kgtw,tkgd->wkd", slope, query_heads, preferred_element_type=f32) * scaling
        )
        block_grads.append(gradient.reshape(local_rows, kv_count * HEAD_DIM))
    attn_out = output_sum.astype(bf16).reshape(local_rows, head_count * HEAD_DIM)
    rotated_grad = block_grads[0]
    for distance in range(1, SPAN + 1):
        rotated_grad = rotated_grad + seq_shift(
            block_grads[distance].astype(bf16), -distance
        ).astype(f32)
    key_grad = rotate(rotated_grad, cosine, -sine).astype(bf16)

    inverse_root = (local_rows * device_count) ** (-0.5)
    hidden_tiles = hidden_seq.reshape(local_rows, lines, 2, HEAD_DIM)
    mine = jnp.where(core == 0, hidden_tiles[:, :, 0], hidden_tiles[:, :, 1])
    theirs = jnp.where(core == 0, hidden_tiles[:, :, 1], hidden_tiles[:, :, 0])

    def term(tiles_of):
        return jnp.einsum(
            "td,tc->dc", tiles_of.reshape(local_rows, -1), key_grad, preferred_element_type=f32
        )

    from_other = core_swap(term(theirs).astype(bf16))
    summed = (term(mine) + from_other.astype(f32)).astype(bf16)
    pieces = jnp.transpose(
        summed.reshape(2, half, seq_count // 2, 8, kv_width), (2, 0, 3, 1, 4)
    ).reshape(seq_count, 8, half * kv_width)
    plane = jnp.sum(exchange(pieces, SEQ).astype(f32), axis=0)
    plane = jnp.transpose(plane.reshape(2, 4, half, kv_width), (2, 0, 1, 3))
    side = lax.axis_index("xl")
    empty = jnp.zeros_like(plane)
    last = jnp.stack([jnp.where(side == 0, plane, empty), jnp.where(side == 1, plane, empty)])
    weight_grad = jnp.sum(
        exchange(last.reshape(2 * lines, 4, kv_width), ("y", "xl")), axis=0
    ) * inverse_root
    return (attn_out, token_loss, weight_grad)


def solution(mesh):
    fine = Mesh(np.asarray(mesh.devices).reshape(8, 2, 8, 2, 2), EVERY)
    pack = ("y", "core")
    placed = (
        P(EVERY, None),
        P(EVERY, None),
        P(EVERY, None),
        P(EVERY),
        P(EVERY, None),
        P(pack, None),
        P(EVERY, None),
        P(EVERY, None),
    )
    return jax.shard_map(
        local,
        mesh=fine,
        in_specs=placed,
        out_specs=(P(EVERY, None), P(EVERY), P(EVERY, None)),
        check_vma=False,
    )
```

```python
import jax
import jax.numpy as jnp
import numpy as np
from jax import lax
from jax.experimental import pallas as pl
from jax.experimental.pallas import tpu as pltpu
from jax.sharding import Mesh
from jax.sharding import PartitionSpec as P

HEAD_DIM = 128
SPAN = 2
SLOTS = 6

negative = -1e30
rope_base = 500000.0

SEQ = ("z", "xh", "xl")
EVERY = ("y", "core") + SEQ


def exchange(pieces, axes):
    return lax.all_to_all(pieces, axes, split_axis=0, concat_axis=0, tiled=True)


def seq_shift(shard, by):
    devices = lax.axis_size(SEQ)
    pairs = [(i, i + by) for i in range(devices) if 0 <= i + by < devices]
    return lax.ppermute(shard, SEQ, pairs)


def line_shift(shard, by):
    devices = lax.axis_size("y")
    return lax.ppermute(shard, "y", [(i, (i + by) % devices) for i in range(devices)])


def core_swap(shard):
    return lax.ppermute(shard, "core", [(0, 1), (1, 0)])


def turn_angles(positions):
    halfway = HEAD_DIM // 2
    frequency = rope_base ** (-2.0 * jnp.arange(halfway, dtype=jnp.float32) / HEAD_DIM)
    angle = positions.astype(jnp.float32)[:, None] * frequency[None, :]
    return jnp.cos(angle)[:, None, :], jnp.sin(angle)[:, None, :]


def rotate(matrix, cosine, sine):
    count = matrix.shape[0]
    halfway = HEAD_DIM // 2
    split = matrix.reshape(count, -1, HEAD_DIM)
    first_half = split[..., :halfway]
    second_half = split[..., halfway:]
    joined = jnp.concatenate(
        [first_half * cosine - second_half * sine, second_half * cosine + first_half * sine],
        axis=-1,
    )
    return joined.reshape(count, -1)


def dialogue_starts(lengths, positions):
    ending = jnp.cumsum(lengths)
    picked = jnp.where(ending[None, :] <= positions[:, None], lengths[None, :], 0)
    return jnp.sum(picked, axis=1)


def block_targets(label_index, label_prob, key_start, width):
    within = label_index - key_start
    columns = jnp.arange(width, dtype=jnp.int32)
    matches = within[..., None] == columns[None, None, None, :]
    table = jnp.sum(jnp.where(matches, label_prob[..., None], 0.0), axis=2)
    return jnp.transpose(table, (1, 0, 2))


def pack_kernel(target_ref, hidden_ref, queries_ref, values_ref, out_ref):
    bf16, f32 = jnp.bfloat16, jnp.float32
    rows = hidden_ref.shape[0]
    parcels = out_ref.shape[0]
    main = out_ref.shape[1] // HEAD_DIM - 1
    third = main // 3
    refs = (hidden_ref, queries_ref, values_ref)
    tiles = [ref[:, i * HEAD_DIM : (i + 1) * HEAD_DIM] for ref in refs for i in range(ref.shape[1] // HEAD_DIM)]
    target = target_ref[...]
    block = target // rows
    offset = (target - block * rows - rows).astype(f32)
    across = jnp.broadcast_to(block.astype(f32), (rows, rows))
    down = across.T
    first = lax.broadcasted_iota(jnp.int32, (rows, rows), 0)
    second = lax.broadcasted_iota(jnp.int32, (rows, rows), 1)
    rank = jnp.sum(jnp.where((across == down) & (first < second), 1.0, 0.0), axis=0, keepdims=True)
    rank = rank.astype(jnp.int32)
    row = lax.broadcasted_iota(jnp.int32, (parcels, rows), 0)
    place = row % 8
    to_block = block == row // 8
    low = jnp.where(to_block & (place == rank) & (place < SLOTS), 1.0, 0.0)
    lane = lax.broadcasted_iota(jnp.int32, (parcels, HEAD_DIM), 1)
    meta = jnp.zeros((parcels, HEAD_DIM), f32)
    extras = jnp.concatenate(tiles[main:], axis=1)
    for m in range(3):
        high = jnp.where(
            to_block & (place - SLOTS + 2 * m == rank) & (place >= SLOTS), 1.0, 0.0
        )
        place_of = jnp.sum((low + high) * offset, axis=1, keepdims=True) + rows
        meta = jnp.where(lane == m, place_of, meta)
        select = jnp.concatenate([low, high], axis=1).astype(bf16)
        both = jnp.concatenate([jnp.concatenate(tiles[m:main:3], axis=1), extras], axis=0)
        done = jnp.dot(select, both, preferred_element_type=f32).astype(bf16)
        for i in range(third):
            g = 3 * i + m
            out_ref[:, g * HEAD_DIM : (g + 1) * HEAD_DIM] = done[:, i * HEAD_DIM : (i + 1) * HEAD_DIM]
    out_ref[:, main * HEAD_DIM :] = meta.astype(bf16)


def unpack_kernel(
    place_ref, got_ref, mine_ref, theirs_ref, mine_turned, theirs_turned, queries_ref, values_ref
):
    bf16, f32 = jnp.bfloat16, jnp.float32
    rows = queries_ref.shape[0]
    parcels = got_ref.shape[0]
    main = got_ref.shape[1] // HEAD_DIM - 1
    third = main // 3
    meta = got_ref[:, main * HEAD_DIM :].astype(f32).T
    token = lax.broadcasted_iota(jnp.int32, (rows, parcels), 0).astype(f32)
    low = lax.broadcasted_iota(jnp.int32, (rows, parcels), 1) % 8 < SLOTS
    tiles = [None] * (main + third)
    extras = jnp.zeros((rows, third * HEAD_DIM), f32)
    for m in range(3):
        hit = meta[m : m + 1, :] == token
        select = jnp.concatenate(
            [jnp.where(hit & low, 1.0, 0.0), jnp.where(hit & ~low, 1.0, 0.0)], axis=0
        ).astype(bf16)
        part = jnp.concatenate(
            [got_ref[:, g * HEAD_DIM : (g + 1) * HEAD_DIM] for g in range(m, main, 3)], axis=1
        )
        done = jnp.dot(select, part, preferred_element_type=f32)
        for i in range(third):
            tiles[3 * i + m] = done[:rows, i * HEAD_DIM : (i + 1) * HEAD_DIM].astype(bf16)
        extras = extras + done[rows:]
    for i in range(third):
        tiles[main + i] = extras[:, i * HEAD_DIM : (i + 1) * HEAD_DIM].astype(bf16)
    hidden_tiles = mine_ref.shape[1] // HEAD_DIM * 2
    query_tiles = queries_ref.shape[1] // HEAD_DIM
    for i in range(query_tiles):
        queries_ref[:, i * HEAD_DIM : (i + 1) * HEAD_DIM] = tiles[hidden_tiles + i]
    for i in range(values_ref.shape[1] // HEAD_DIM):
        values_ref[:, i * HEAD_DIM : (i + 1) * HEAD_DIM] = tiles[hidden_tiles + query_tiles + i]
    is_first = jnp.broadcast_to(place_ref[0], (rows, HEAD_DIM)) == 0
    count = hidden_tiles // 2
    for i in range(count):
        even, odd = tiles[2 * i].astype(f32), tiles[2 * i + 1].astype(f32)
        own = jnp.where(is_first, even, odd).astype(bf16)
        other = jnp.where(is_first, odd, even).astype(bf16)
        mine_ref[:, i * HEAD_DIM : (i + 1) * HEAD_DIM] = own
        theirs_ref[:, i * HEAD_DIM : (i + 1) * HEAD_DIM] = other
        turned = lax.rem(place_ref[1] - i + count, count)
        lanes = pl.ds(pl.multiple_of(turned * HEAD_DIM, HEAD_DIM), HEAD_DIM)
        mine_turned[:, lanes] = own
        theirs_turned[:, lanes] = other


def whole(count=1):
    return [pl.BlockSpec(memory_space=pltpu.VMEM)] * count


def pack_rows(hidden, queries, values, row_target, seq_count):
    rows = hidden.shape[0]
    tiles = (hidden.shape[1] + queries.shape[1] + values.shape[1]) // HEAD_DIM
    main = tiles - tiles // 4
    return pl.pallas_call(
        pack_kernel,
        out_shape=jax.ShapeDtypeStruct((seq_count * 8, (main + 1) * HEAD_DIM), jnp.bfloat16),
        in_specs=whole(4),
        out_specs=whole()[0],
        name="pack_rows",
    )(row_target.reshape(1, rows), hidden, queries, values)


def unpack_rows(got, place_of, rows, width, kv_width):
    shapes = [(rows, width // 2)] * 4 + [(rows, width), (rows, kv_width)]
    return pl.pallas_call(
        unpack_kernel,
        out_shape=[jax.ShapeDtypeStruct(s, jnp.bfloat16) for s in shapes],
        in_specs=[pl.BlockSpec(memory_space=pltpu.SMEM)] + whole(),
        out_specs=whole(6),
        name="unpack_rows",
    )(place_of, got)


def local(
    hidden, queries, values, row_target, key_weight, dialogue_lengths, teacher_pick, teacher_prob
):
    bf16, f32 = jnp.bfloat16, jnp.float32
    local_rows, width = hidden.shape
    seq_count = lax.axis_size(SEQ)
    seq_index = lax.axis_index(SEQ)
    lines = lax.axis_size("y")
    device_count = seq_count * lines * lax.axis_size("core")
    head_count = queries.shape[1] // HEAD_DIM
    kv_width = values.shape[1]
    kv_count = kv_width // HEAD_DIM
    group_size = head_count // kv_count
    top_count = teacher_pick.shape[1] // head_count
    scaling = HEAD_DIM ** (-0.5)

    place_of = jnp.stack([lax.axis_index("core"), lax.axis_index("y")]).astype(jnp.int32)

    plane_rows = exchange(jnp.broadcast_to(key_weight, (seq_count,) + key_weight.shape), SEQ)
    plane_rows = plane_rows.reshape(local_rows, kv_width)
    own_half = jnp.concatenate(
        [plane_rows] + [line_shift(plane_rows, by) for by in range(1, lines)], axis=0
    )
    other_half = core_swap(own_half)

    parcels = pack_rows(hidden, queries, values, row_target, seq_count)
    received = exchange(parcels.reshape(seq_count, 8, -1), SEQ)
    mine, theirs, mine_turned, theirs_turned, queries_seq, values_seq = unpack_rows(
        received.reshape(seq_count * 8, -1), place_of, local_rows, width, kv_width
    )

    positions = seq_index * local_rows + jnp.arange(local_rows, dtype=jnp.int32)
    cosine, sine = turn_angles(positions)
    keys_seq = rotate(
        jnp.dot(mine_turned, own_half, preferred_element_type=f32)
        + jnp.dot(theirs_turned, other_half, preferred_element_type=f32),
        cosine,
        sine,
    ).astype(bf16)
    starts = dialogue_starts(dialogue_lengths[0], positions)
    reach = (positions - starts + 1)[:, None]
    label_index = (starts[:, None] + teacher_pick % reach).reshape(
        local_rows, head_count, top_count
    )
    label_prob = teacher_prob.reshape(local_rows, head_count, top_count)
    target_mass = jnp.sum(label_prob, axis=2).T.reshape(kv_count, group_size, local_rows)
    entropy = jnp.sum(label_prob * jnp.log(label_prob), axis=(1, 2))
    query_heads = queries_seq.reshape(local_rows, kv_count, group_size, HEAD_DIM)
    blocks = [(keys_seq, values_seq)]
    for distance in range(1, SPAN + 1):
        blocks.append((seq_shift(keys_seq, distance), seq_shift(values_seq, distance)))

    def scores_of(key_block, key_start):
        key_heads = key_block.reshape(local_rows, kv_count, HEAD_DIM)
        score = (
            jnp.einsum("tkgd,wkd->kgtw", query_heads, key_heads, preferred_element_type=f32)
            * scaling
        )
        key_pos = key_start + jnp.arange(local_rows, dtype=jnp.int32)
        allowed = (key_pos[None, :] >= starts[:, None]) & (key_pos[None, :] <= positions[:, None])
        held = jnp.where(allowed[None, None], score, negative)
        table = block_targets(label_index, label_prob, key_start, local_rows)
        return (score, held, table.reshape(kv_count, group_size, local_rows, local_rows))

    tops, totals, pickings = ([], [], [])
    for distance, (key_block, value_block) in enumerate(blocks):
        key_start = (seq_index - distance) * local_rows
        score, held, table = scores_of(key_block, key_start)
        block_top = jnp.max(held, axis=-1)
        tops.append(block_top)
        totals.append(jnp.sum(jnp.exp(held - block_top[..., None]), axis=-1))
        pickings.append(jnp.sum(table * score, axis=-1))
    top_all = jnp.max(jnp.stack(tops), axis=0)
    total_all = jnp.sum(jnp.stack(totals) * jnp.exp(jnp.stack(tops) - top_all[None]), axis=0)
    lse = top_all + jnp.log(total_all)
    picked_all = jnp.sum(jnp.stack(pickings), axis=0)
    token_loss = (
        entropy - jnp.sum(picked_all, axis=(0, 1)) + jnp.sum(target_mass * lse, axis=(0, 1))
    ) / head_count

    output_sum = jnp.zeros((local_rows, kv_count, group_size, HEAD_DIM), f32)
    block_grads = []
    for distance, (key_block, value_block) in enumerate(blocks):
        key_start = (seq_index - distance) * local_rows
        score, held, table = scores_of(key_block, key_start)
        weight_of = jnp.exp(held - lse[..., None])
        value_heads = value_block.reshape(local_rows, kv_count, HEAD_DIM)
        output_sum = output_sum + jnp.einsum(
            "kgtw,wkd->tkgd", weight_of.astype(bf16), value_heads, preferred_element_type=f32
        )
        slope = ((weight_of * target_mass[..., None] - table) / head_count).astype(bf16)
        gradient = (
            jnp.einsum("kgtw,tkgd->wkd", slope, query_heads, preferred_element_type=f32) * scaling
        )
        block_grads.append(gradient.reshape(local_rows, kv_count * HEAD_DIM))
    attn_out = output_sum.astype(bf16).reshape(local_rows, head_count * HEAD_DIM)
    rotated_grad = block_grads[0]
    for distance in range(1, SPAN + 1):
        rotated_grad = rotated_grad + seq_shift(
            block_grads[distance].astype(bf16), -distance
        ).astype(f32)
    key_grad = rotate(rotated_grad, cosine, -sine).astype(bf16)

    inverse_root = (local_rows * device_count) ** (-0.5)
    def term(tiles_of):
        return jnp.einsum(
            "td,tc->dc", tiles_of, key_grad, preferred_element_type=f32
        )

    from_other = core_swap(term(theirs).astype(bf16))
    summed = (term(mine) + from_other.astype(f32)).astype(bf16)
    half = lines // 2
    depth = lax.axis_size("z")
    pieces = jnp.transpose(
        summed.reshape(2, half, depth, 2, 8, kv_width), (3, 0, 2, 1, 4, 5)
    ).reshape(4, depth * half * 8, kv_width)
    line = jnp.sum(exchange(pieces, ("xh", "xl")).astype(f32), axis=0).astype(bf16)
    line = line.reshape(depth, half * 8, kv_width)
    plane = jnp.sum(exchange(line, "z").astype(f32), axis=0)
    plane = plane.reshape(half, 2, 4, kv_width)
    side = lax.axis_index("xl")
    empty = jnp.zeros_like(plane)
    last = jnp.stack([jnp.where(side == 0, plane, empty), jnp.where(side == 1, plane, empty)])
    weight_grad = jnp.sum(
        exchange(last.reshape(2 * lines, 4, kv_width), ("y", "xl")), axis=0
    ) * inverse_root
    return (attn_out, token_loss, weight_grad)


def solution(mesh):
    fine = Mesh(np.asarray(mesh.devices).reshape(8, 2, 8, 2, 2), EVERY)
    pack = ("y", "core")
    placed = (
        P(EVERY, None),
        P(EVERY, None),
        P(EVERY, None),
        P(EVERY),
        P(EVERY, None),
        P(pack, None),
        P(EVERY, None),
        P(EVERY, None),
    )
    return jax.shard_map(
        local,
        mesh=fine,
        in_specs=placed,
        out_specs=(P(EVERY, None), P(EVERY), P(EVERY, None)),
        check_vma=False,
    )
```

```python
import jax
import jax.numpy as jnp
import numpy as np
from jax import lax
from jax.experimental import pallas as pl
from jax.experimental.pallas import tpu as pltpu
from jax.sharding import Mesh
from jax.sharding import PartitionSpec as P

HEAD_DIM = 128
SPAN = 2
SLOTS = 6

negative = -1e30
rope_base = 500000.0

SEQ = ("z", "xh", "xl")
EVERY = ("y", "core") + SEQ


def exchange(pieces, axes):
    return lax.all_to_all(pieces, axes, split_axis=0, concat_axis=0, tiled=True)


def seq_shift(shard, by):
    devices = lax.axis_size(SEQ)
    pairs = [(i, i + by) for i in range(devices) if 0 <= i + by < devices]
    return lax.ppermute(shard, SEQ, pairs)


def line_shift(shard, by):
    devices = lax.axis_size("y")
    return lax.ppermute(shard, "y", [(i, (i + by) % devices) for i in range(devices)])


def core_swap(shard):
    return lax.ppermute(shard, "core", [(0, 1), (1, 0)])


def turn_angles(positions):
    halfway = HEAD_DIM // 2
    frequency = rope_base ** (-2.0 * jnp.arange(halfway, dtype=jnp.float32) / HEAD_DIM)
    angle = positions.astype(jnp.float32)[:, None] * frequency[None, :]
    return jnp.cos(angle)[:, None, :], jnp.sin(angle)[:, None, :]


def rotate(matrix, cosine, sine):
    count = matrix.shape[0]
    halfway = HEAD_DIM // 2
    split = matrix.reshape(count, -1, HEAD_DIM)
    first_half = split[..., :halfway]
    second_half = split[..., halfway:]
    joined = jnp.concatenate(
        [first_half * cosine - second_half * sine, second_half * cosine + first_half * sine],
        axis=-1,
    )
    return joined.reshape(count, -1)


def dialogue_starts(lengths, positions):
    ending = jnp.cumsum(lengths)
    picked = jnp.where(ending[None, :] <= positions[:, None], lengths[None, :], 0)
    return jnp.sum(picked, axis=1)


def pack_kernel(target_ref, hidden_ref, queries_ref, values_ref, out_ref):
    bf16, f32 = jnp.bfloat16, jnp.float32
    rows = hidden_ref.shape[0]
    parcels = out_ref.shape[0]
    main = out_ref.shape[1] // HEAD_DIM - 1
    third = main // 3
    refs = (hidden_ref, queries_ref, values_ref)
    tiles = [ref[:, i * HEAD_DIM : (i + 1) * HEAD_DIM] for ref in refs for i in range(ref.shape[1] // HEAD_DIM)]
    target = target_ref[...]
    block = target // rows
    offset = (target - block * rows - rows).astype(f32)
    across = jnp.broadcast_to(block.astype(f32), (rows, rows))
    down = across.T
    first = lax.broadcasted_iota(jnp.int32, (rows, rows), 0)
    second = lax.broadcasted_iota(jnp.int32, (rows, rows), 1)
    rank = jnp.sum(jnp.where((across == down) & (first < second), 1.0, 0.0), axis=0, keepdims=True)
    rank = rank.astype(jnp.int32)
    row = lax.broadcasted_iota(jnp.int32, (parcels, rows), 0)
    place = row % 8
    to_block = block == row // 8
    low = jnp.where(to_block & (place == rank) & (place < SLOTS), 1.0, 0.0)
    lane = lax.broadcasted_iota(jnp.int32, (parcels, HEAD_DIM), 1)
    meta = jnp.zeros((parcels, HEAD_DIM), f32)
    extras = jnp.concatenate(tiles[main:], axis=1)
    for m in range(3):
        high = jnp.where(
            to_block & (place - SLOTS + 2 * m == rank) & (place >= SLOTS), 1.0, 0.0
        )
        place_of = jnp.sum((low + high) * offset, axis=1, keepdims=True) + rows
        meta = jnp.where(lane == m, place_of, meta)
        select = jnp.concatenate([low, high], axis=1).astype(bf16)
        both = jnp.concatenate([jnp.concatenate(tiles[m:main:3], axis=1), extras], axis=0)
        done = jnp.dot(select, both, preferred_element_type=f32).astype(bf16)
        for i in range(third):
            g = 3 * i + m
            out_ref[:, g * HEAD_DIM : (g + 1) * HEAD_DIM] = done[:, i * HEAD_DIM : (i + 1) * HEAD_DIM]
    out_ref[:, main * HEAD_DIM :] = meta.astype(bf16)


def unpack_kernel(
    place_ref, got_ref, mine_ref, theirs_ref, mine_turned, theirs_turned, queries_ref, values_ref
):
    bf16, f32 = jnp.bfloat16, jnp.float32
    rows = queries_ref.shape[0]
    parcels = got_ref.shape[0]
    main = got_ref.shape[1] // HEAD_DIM - 1
    third = main // 3
    meta = got_ref[:, main * HEAD_DIM :].astype(f32).T
    token = lax.broadcasted_iota(jnp.int32, (rows, parcels), 0).astype(f32)
    low = lax.broadcasted_iota(jnp.int32, (rows, parcels), 1) % 8 < SLOTS
    tiles = [None] * (main + third)
    extras = jnp.zeros((rows, third * HEAD_DIM), f32)
    for m in range(3):
        hit = meta[m : m + 1, :] == token
        select = jnp.concatenate(
            [jnp.where(hit & low, 1.0, 0.0), jnp.where(hit & ~low, 1.0, 0.0)], axis=0
        ).astype(bf16)
        part = jnp.concatenate(
            [got_ref[:, g * HEAD_DIM : (g + 1) * HEAD_DIM] for g in range(m, main, 3)], axis=1
        )
        done = jnp.dot(select, part, preferred_element_type=f32)
        for i in range(third):
            tiles[3 * i + m] = done[:rows, i * HEAD_DIM : (i + 1) * HEAD_DIM].astype(bf16)
        extras = extras + done[rows:]
    for i in range(third):
        tiles[main + i] = extras[:, i * HEAD_DIM : (i + 1) * HEAD_DIM].astype(bf16)
    hidden_tiles = mine_ref.shape[1] // HEAD_DIM * 2
    query_tiles = queries_ref.shape[1] // HEAD_DIM
    for i in range(query_tiles):
        queries_ref[:, i * HEAD_DIM : (i + 1) * HEAD_DIM] = tiles[hidden_tiles + i]
    for i in range(values_ref.shape[1] // HEAD_DIM):
        values_ref[:, i * HEAD_DIM : (i + 1) * HEAD_DIM] = tiles[hidden_tiles + query_tiles + i]
    is_first = jnp.broadcast_to(place_ref[0], (rows, HEAD_DIM)) == 0
    count = hidden_tiles // 2
    for i in range(count):
        even, odd = tiles[2 * i].astype(f32), tiles[2 * i + 1].astype(f32)
        own = jnp.where(is_first, even, odd).astype(bf16)
        other = jnp.where(is_first, odd, even).astype(bf16)
        mine_ref[:, i * HEAD_DIM : (i + 1) * HEAD_DIM] = own
        theirs_ref[:, i * HEAD_DIM : (i + 1) * HEAD_DIM] = other
        turned = lax.rem(place_ref[1] - i + count, count)
        lanes = pl.ds(pl.multiple_of(turned * HEAD_DIM, HEAD_DIM), HEAD_DIM)
        mine_turned[:, lanes] = own
        theirs_turned[:, lanes] = other


def attend_kernel(
    start_ref, q_ref, k0_ref, k1_ref, k2_ref, pick_ref, prob_ref,
    g0_ref, g1_ref, g2_ref, loss_ref, weight_ref, spot_scr, prob_scr,
):
    bf16, f32 = jnp.bfloat16, jnp.float32
    rows = q_ref.shape[0]
    kv_count = k0_ref.shape[1] // HEAD_DIM
    heads = q_ref.shape[1] // HEAD_DIM
    group = heads // kv_count
    top = pick_ref.shape[1] // heads
    window = SPAN * rows
    scaling = HEAD_DIM ** (-0.5)
    query = lax.broadcasted_iota(jnp.int32, (1, rows), 1).astype(f32)
    start = start_ref[...].astype(f32)
    reach = query - start + 1.0
    picked = pick_ref[...].astype(f32).T
    rest = picked - jnp.floor(picked / reach) * reach
    rest = jnp.where(rest < 0.0, rest + reach, rest)
    rest = jnp.where(rest >= reach, rest - reach, rest)
    spot = start + rest
    spot_scr[...] = jnp.where(spot < 0.0, spot + window, spot)
    prob_all = prob_ref[...].T
    prob_scr[...] = prob_all
    entropy = jnp.sum(prob_all * jnp.log(prob_all), axis=0, keepdims=True)
    spots = lax.broadcasted_iota(jnp.int32, (window, rows), 0).astype(f32)
    across = lax.broadcasted_iota(jnp.int32, (window, rows), 1).astype(f32)
    position = jnp.where(spots <= across, spots, spots - window)
    allowed = position >= start
    near = spots[:rows] <= across[:rows]

    def parted(rows_of):
        low = rows_of[:rows]
        return jnp.concatenate(
            [jnp.where(near, low, 0.0), jnp.where(near, 0.0, low), rows_of[rows:]], axis=0
        ).astype(bf16)

    def one_group(g, loss):
        lanes = pl.ds(pl.multiple_of(g * HEAD_DIM, HEAD_DIM), HEAD_DIM)
        queries = jnp.concatenate(
            [
                q_ref[:, pl.ds(pl.multiple_of((g * group + i) * HEAD_DIM, HEAD_DIM), HEAD_DIM)]
                for i in range(group)
            ],
            axis=0,
        )
        keys = jnp.concatenate([k0_ref[:, lanes], k2_ref[:, lanes], k1_ref[:, lanes]], axis=0)
        dots = lax.dot_general(
            keys, queries, (((1,), (1,)), ((), ())), preferred_element_type=f32
        )
        slopes = []
        for i in range(group):
            mine = dots[:, i * rows : (i + 1) * rows]
            score = (
                jnp.concatenate(
                    [jnp.where(near, mine[:rows], mine[rows : 2 * rows]), mine[2 * rows :]], axis=0
                )
                * scaling
            )
            held = jnp.where(allowed, score, negative)
            peak = jnp.max(held, axis=0, keepdims=True)
            raised = jnp.exp(held - peak)
            total = jnp.sum(raised, axis=0, keepdims=True)
            weight = raised * (1.0 / total)
            labels = pl.ds(pl.multiple_of((g * group + i) * top, top), top)
            spot_rows, prob_rows = spot_scr[labels, :], prob_scr[labels, :]
            table = jnp.zeros((window, rows), f32)
            for k in range(top):
                table = table + jnp.where(
                    spots == spot_rows[k : k + 1], prob_rows[k : k + 1], 0.0
                )
            mass = jnp.sum(prob_rows, axis=0, keepdims=True)
            loss = loss + mass * (peak + jnp.log(total))
            loss = loss - jnp.sum(table * score, axis=0, keepdims=True)
            weight_ref[g, :, i * rows : (i + 1) * rows] = parted(weight)
            slopes.append(parted((weight * mass - table) * (1.0 / heads)))
        grads = jnp.dot(
            jnp.concatenate(slopes, axis=1), queries, preferred_element_type=f32
        ) * scaling
        g0_ref[:, lanes] = grads[:rows]
        g2_ref[:, lanes] = grads[rows : 2 * rows].astype(bf16)
        g1_ref[:, lanes] = grads[2 * rows :].astype(bf16)
        return loss

    loss = lax.fori_loop(0, kv_count, one_group, entropy)
    loss_ref[...] = loss * (1.0 / heads)


def output_kernel(weight_ref, v0_ref, v1_ref, v2_ref, out_ref):
    bf16, f32 = jnp.bfloat16, jnp.float32
    rows = v0_ref.shape[0]
    group = weight_ref.shape[2] // rows
    for g in range(weight_ref.shape[0]):
        lanes = slice(g * HEAD_DIM, (g + 1) * HEAD_DIM)
        values = jnp.concatenate([v0_ref[:, lanes], v2_ref[:, lanes], v1_ref[:, lanes]], axis=0)
        flipped = jnp.dot(
            values.astype(f32).T.astype(bf16), weight_ref[g], preferred_element_type=f32
        )
        for i in range(group):
            h = g * group + i
            out_ref[:, h * HEAD_DIM : (h + 1) * HEAD_DIM] = (
                flipped[:, i * rows : (i + 1) * rows].T.astype(bf16)
            )


def attend(start, queries, keys, pick, prob):
    rows, kv_width = keys[0].shape
    kv_count = kv_width // HEAD_DIM
    group = queries.shape[1] // kv_width
    bf16, f32 = jnp.bfloat16, jnp.float32
    struct = jax.ShapeDtypeStruct
    return pl.pallas_call(
        attend_kernel,
        out_shape=[
            struct((rows, kv_width), f32),
            struct((rows, kv_width), bf16),
            struct((rows, kv_width), bf16),
            struct((1, rows), f32),
            struct((kv_count, (SPAN + 1) * rows, group * rows), bf16),
        ],
        in_specs=whole(7),
        out_specs=whole(5),
        scratch_shapes=[pltpu.VMEM(pick.shape[::-1], f32)] * 2,
        name="attend",
    )(start.reshape(1, rows), queries, *keys, pick, prob)


def attend_output(weights, values):
    rows = values[0].shape[0]
    heads = weights.shape[0] * weights.shape[2] // rows
    return pl.pallas_call(
        output_kernel,
        out_shape=jax.ShapeDtypeStruct((rows, heads * HEAD_DIM), jnp.bfloat16),
        in_specs=whole(4),
        out_specs=whole()[0],
        name="attend_output",
    )(weights, *values)


def whole(count=1):
    return [pl.BlockSpec(memory_space=pltpu.VMEM)] * count


def pack_rows(hidden, queries, values, row_target, seq_count):
    rows = hidden.shape[0]
    tiles = (hidden.shape[1] + queries.shape[1] + values.shape[1]) // HEAD_DIM
    main = tiles - tiles // 4
    return pl.pallas_call(
        pack_kernel,
        out_shape=jax.ShapeDtypeStruct((seq_count * 8, (main + 1) * HEAD_DIM), jnp.bfloat16),
        in_specs=whole(4),
        out_specs=whole()[0],
        name="pack_rows",
    )(row_target.reshape(1, rows), hidden, queries, values)


def unpack_rows(got, place_of, rows, width, kv_width):
    shapes = [(rows, width // 2)] * 4 + [(rows, width), (rows, kv_width)]
    return pl.pallas_call(
        unpack_kernel,
        out_shape=[jax.ShapeDtypeStruct(s, jnp.bfloat16) for s in shapes],
        in_specs=[pl.BlockSpec(memory_space=pltpu.SMEM)] + whole(),
        out_specs=whole(6),
        name="unpack_rows",
    )(place_of, got)


def local(
    hidden, queries, values, row_target, key_weight, dialogue_lengths, teacher_pick, teacher_prob
):
    bf16, f32 = jnp.bfloat16, jnp.float32
    local_rows, width = hidden.shape
    seq_count = lax.axis_size(SEQ)
    seq_index = lax.axis_index(SEQ)
    lines = lax.axis_size("y")
    device_count = seq_count * lines * lax.axis_size("core")
    kv_width = values.shape[1]

    place_of = jnp.stack([lax.axis_index("core"), lax.axis_index("y")]).astype(jnp.int32)

    plane_rows = exchange(jnp.broadcast_to(key_weight, (seq_count,) + key_weight.shape), SEQ)
    plane_rows = plane_rows.reshape(local_rows, kv_width)
    own_half = jnp.concatenate(
        [plane_rows] + [line_shift(plane_rows, by) for by in range(1, lines)], axis=0
    )
    other_half = core_swap(own_half)

    parcels = pack_rows(hidden, queries, values, row_target, seq_count)
    received = exchange(parcels.reshape(seq_count, 8, -1), SEQ)
    mine, theirs, mine_turned, theirs_turned, queries_seq, values_seq = unpack_rows(
        received.reshape(seq_count * 8, -1), place_of, local_rows, width, kv_width
    )

    positions = seq_index * local_rows + jnp.arange(local_rows, dtype=jnp.int32)
    cosine, sine = turn_angles(positions)
    keys_seq = rotate(
        jnp.dot(mine_turned, own_half, preferred_element_type=f32)
        + jnp.dot(theirs_turned, other_half, preferred_element_type=f32),
        cosine,
        sine,
    ).astype(bf16)
    starts = dialogue_starts(dialogue_lengths[0], positions)
    keys = [keys_seq] + [seq_shift(keys_seq, by) for by in range(1, SPAN + 1)]
    values_near = [values_seq] + [seq_shift(values_seq, by) for by in range(1, SPAN + 1)]
    own_grad, grad_1, grad_2, token_loss, weights = attend(
        starts - seq_index * local_rows, queries_seq, keys, teacher_pick, teacher_prob
    )
    grad_1, grad_2, values_1, values_2 = lax.optimization_barrier(
        (grad_1, grad_2, values_near[1], values_near[2])
    )
    attn_out = attend_output(weights, (values_seq, values_1, values_2))
    rotated_grad = (
        own_grad + seq_shift(grad_1, -1).astype(f32) + seq_shift(grad_2, -2).astype(f32)
    )
    key_grad = rotate(rotated_grad, cosine, -sine).astype(bf16)

    inverse_root = (local_rows * device_count) ** (-0.5)
    def term(tiles_of):
        return jnp.einsum(
            "td,tc->dc", tiles_of, key_grad, preferred_element_type=f32
        )

    from_other = core_swap(term(theirs).astype(bf16))
    summed = (term(mine) + from_other.astype(f32)).astype(bf16)
    half = lines // 2
    depth = lax.axis_size("z")
    pieces = jnp.transpose(
        summed.reshape(2, half, depth, 2, 8, kv_width), (3, 0, 2, 1, 4, 5)
    ).reshape(4, depth * half * 8, kv_width)
    line = jnp.sum(exchange(pieces, ("xh", "xl")).astype(f32), axis=0).astype(bf16)
    line = line.reshape(depth, half * 8, kv_width)
    plane = jnp.sum(exchange(line, "z").astype(f32), axis=0)
    plane = plane.reshape(half, 2, 4, kv_width)
    side = lax.axis_index("xl")
    empty = jnp.zeros_like(plane)
    last = jnp.stack([jnp.where(side == 0, plane, empty), jnp.where(side == 1, plane, empty)])
    weight_grad = jnp.sum(
        exchange(last.reshape(2 * lines, 4, kv_width), ("y", "xl")), axis=0
    ) * inverse_root
    return (attn_out, token_loss.reshape(local_rows), weight_grad)


def solution(mesh):
    fine = Mesh(np.asarray(mesh.devices).reshape(8, 2, 8, 2, 2), EVERY)
    pack = ("y", "core")
    placed = (
        P(EVERY, None),
        P(EVERY, None),
        P(EVERY, None),
        P(EVERY),
        P(EVERY, None),
        P(pack, None),
        P(EVERY, None),
        P(EVERY, None),
    )
    return jax.shard_map(
        local,
        mesh=fine,
        in_specs=placed,
        out_specs=(P(EVERY, None), P(EVERY), P(EVERY, None)),
        check_vma=False,
    )
```

```python
import jax
import jax.numpy as jnp
import numpy as np
from jax import lax
from jax.experimental import pallas as pl
from jax.experimental.pallas import tpu as pltpu
from jax.sharding import Mesh
from jax.sharding import PartitionSpec as P

HEAD_DIM = 128
SPAN = 2
SLOTS = 6

negative = -1e30
rope_base = 500000.0

GRANT = pltpu.CompilerParams(vmem_limit_bytes=24 << 20)

SEQ = ("z", "xh", "xl")
EVERY = ("y", "core") + SEQ


def exchange(pieces, axes):
    return lax.all_to_all(pieces, axes, split_axis=0, concat_axis=0, tiled=True)


def seq_shift(shard, by):
    devices = lax.axis_size(SEQ)
    pairs = [(i, i + by) for i in range(devices) if 0 <= i + by < devices]
    return lax.ppermute(shard, SEQ, pairs)


def line_shift(shard, by):
    devices = lax.axis_size("y")
    return lax.ppermute(shard, "y", [(i, (i + by) % devices) for i in range(devices)])


def core_swap(shard):
    return lax.ppermute(shard, "core", [(0, 1), (1, 0)])


def turn_angles(positions):
    halfway = HEAD_DIM // 2
    frequency = rope_base ** (-2.0 * jnp.arange(halfway, dtype=jnp.float32) / HEAD_DIM)
    angle = positions.astype(jnp.float32)[:, None] * frequency[None, :]
    return jnp.cos(angle)[:, None, :], jnp.sin(angle)[:, None, :]


def rotate(matrix, cosine, sine):
    count = matrix.shape[0]
    halfway = HEAD_DIM // 2
    split = matrix.reshape(count, -1, HEAD_DIM)
    first_half = split[..., :halfway]
    second_half = split[..., halfway:]
    joined = jnp.concatenate(
        [first_half * cosine - second_half * sine, second_half * cosine + first_half * sine],
        axis=-1,
    )
    return joined.reshape(count, -1)


def dialogue_starts(lengths, positions):
    ending = jnp.cumsum(lengths)
    picked = jnp.where(ending[None, :] <= positions[:, None], lengths[None, :], 0)
    return jnp.sum(picked, axis=1)


def pack_kernel(target_ref, hidden_ref, queries_ref, values_ref, out_ref):
    bf16, f32 = jnp.bfloat16, jnp.float32
    rows = hidden_ref.shape[0]
    parcels = out_ref.shape[0]
    main = out_ref.shape[1] // HEAD_DIM - 1
    third = main // 3
    refs = (hidden_ref, queries_ref, values_ref)
    tiles = [ref[:, i * HEAD_DIM : (i + 1) * HEAD_DIM] for ref in refs for i in range(ref.shape[1] // HEAD_DIM)]
    target = target_ref[...]
    block = target // rows
    offset = (target - block * rows - rows).astype(f32)
    across = jnp.broadcast_to(block.astype(f32), (rows, rows))
    down = across.T
    first = lax.broadcasted_iota(jnp.int32, (rows, rows), 0)
    second = lax.broadcasted_iota(jnp.int32, (rows, rows), 1)
    rank = jnp.sum(jnp.where((across == down) & (first < second), 1.0, 0.0), axis=0, keepdims=True)
    rank = rank.astype(jnp.int32)
    row = lax.broadcasted_iota(jnp.int32, (parcels, rows), 0)
    place = row % 8
    to_block = block == row // 8
    low = jnp.where(to_block & (place == rank) & (place < SLOTS), 1.0, 0.0)
    lane = lax.broadcasted_iota(jnp.int32, (parcels, HEAD_DIM), 1)
    meta = jnp.zeros((parcels, HEAD_DIM), f32)
    extras = jnp.concatenate(tiles[main:], axis=1)
    for m in range(3):
        high = jnp.where(
            to_block & (place - SLOTS + 2 * m == rank) & (place >= SLOTS), 1.0, 0.0
        )
        place_of = jnp.sum((low + high) * offset, axis=1, keepdims=True) + rows
        meta = jnp.where(lane == m, place_of, meta)
        select = jnp.concatenate([low, high], axis=1).astype(bf16)
        both = jnp.concatenate([jnp.concatenate(tiles[m:main:3], axis=1), extras], axis=0)
        done = jnp.dot(select, both, preferred_element_type=f32).astype(bf16)
        for i in range(third):
            g = 3 * i + m
            out_ref[:, g * HEAD_DIM : (g + 1) * HEAD_DIM] = done[:, i * HEAD_DIM : (i + 1) * HEAD_DIM]
    out_ref[:, main * HEAD_DIM :] = meta.astype(bf16)


def tile_columns(ref, indices):
    return jnp.concatenate([ref[:, g * HEAD_DIM : (g + 1) * HEAD_DIM] for g in indices], axis=1)


def arrivals(got_ref, rows):
    parcels = got_ref.shape[0]
    main = got_ref.shape[1] // HEAD_DIM - 1
    meta = got_ref[:, main * HEAD_DIM :].astype(jnp.float32).T
    token = lax.broadcasted_iota(jnp.int32, (rows, parcels), 0).astype(jnp.float32)
    low = lax.broadcasted_iota(jnp.int32, (rows, parcels), 1) % 8 < SLOTS
    hits = [meta[m : m + 1, :] == token for m in range(3)]
    into = jnp.where(hits[0] & low, 1.0, 0.0).astype(jnp.bfloat16)
    late = [jnp.where(hit & ~low, 1.0, 0.0).astype(jnp.bfloat16) for hit in hits]
    return main, into, late


def hidden_kernel(place_ref, got_ref, mine_ref, theirs_ref, mine_turned, theirs_turned):
    bf16, f32 = jnp.bfloat16, jnp.float32
    rows = mine_ref.shape[0]
    count = mine_ref.shape[1] // HEAD_DIM
    _, into, _ = arrivals(got_ref, rows)
    done = jnp.dot(into, got_ref[:, : 2 * count * HEAD_DIM], preferred_element_type=f32)
    is_first = jnp.broadcast_to(place_ref[0], (rows, HEAD_DIM)) == 0
    for i in range(count):
        even = done[:, 2 * i * HEAD_DIM : (2 * i + 1) * HEAD_DIM]
        odd = done[:, (2 * i + 1) * HEAD_DIM : (2 * i + 2) * HEAD_DIM]
        own = jnp.where(is_first, even, odd).astype(bf16)
        other = jnp.where(is_first, odd, even).astype(bf16)
        mine_ref[:, i * HEAD_DIM : (i + 1) * HEAD_DIM] = own
        theirs_ref[:, i * HEAD_DIM : (i + 1) * HEAD_DIM] = other
        turned = lax.rem(place_ref[1] - i + count, count)
        lanes = pl.ds(pl.multiple_of(turned * HEAD_DIM, HEAD_DIM), HEAD_DIM)
        mine_turned[:, lanes] = own
        theirs_turned[:, lanes] = other


def rest_kernel(got_ref, queries_ref, values_ref):
    bf16, f32 = jnp.bfloat16, jnp.float32
    rows, width = queries_ref.shape
    main, into, late = arrivals(got_ref, rows)
    first = jnp.dot(into, got_ref[:, width : main * HEAD_DIM], preferred_element_type=f32)
    first_width = first.shape[1]
    queries_ref[:, :first_width] = first.astype(bf16)
    extras = jnp.zeros((rows, main // 3 * HEAD_DIM), f32)
    for m in range(3):
        extras = extras + jnp.dot(
            late[m], tile_columns(got_ref, range(m, main, 3)), preferred_element_type=f32
        )
    extras = extras.astype(bf16)
    queries_ref[:, first_width:] = extras[:, : width - first_width]
    values_ref[...] = extras[:, width - first_width :]


def attend_kernel(
    start_ref, q_ref, k0_ref, k1_ref, k2_ref, pick_ref, prob_ref,
    g0_ref, g1_ref, g2_ref, loss_ref, weight_ref, spot_scr, prob_scr,
):
    bf16, f32 = jnp.bfloat16, jnp.float32
    rows = q_ref.shape[0]
    kv_count = k0_ref.shape[1] // HEAD_DIM
    heads = q_ref.shape[1] // HEAD_DIM
    group = heads // kv_count
    top = pick_ref.shape[1] // heads
    window = SPAN * rows
    scaling = HEAD_DIM ** (-0.5)
    query = lax.broadcasted_iota(jnp.int32, (1, rows), 1).astype(f32)
    start = start_ref[...].astype(f32)
    reach = query - start + 1.0
    picked = pick_ref[...].astype(f32).T
    rest = picked - jnp.floor(picked / reach) * reach
    rest = jnp.where(rest < 0.0, rest + reach, rest)
    rest = jnp.where(rest >= reach, rest - reach, rest)
    spot = start + rest
    spot_scr[...] = jnp.where(spot < 0.0, spot + window, spot)
    prob_all = prob_ref[...].T
    prob_scr[...] = prob_all
    entropy = jnp.sum(prob_all * jnp.log(prob_all), axis=0, keepdims=True)
    spots = lax.broadcasted_iota(jnp.int32, (window, rows), 0).astype(f32)
    across = lax.broadcasted_iota(jnp.int32, (window, rows), 1).astype(f32)
    position = jnp.where(spots <= across, spots, spots - window)
    allowed = position >= start
    near = spots[:rows] <= across[:rows]

    def parted(rows_of):
        low = rows_of[:rows]
        return jnp.concatenate(
            [jnp.where(near, low, 0.0), jnp.where(near, 0.0, low), rows_of[rows:]], axis=0
        ).astype(bf16)

    def one_group(g, loss):
        lanes = pl.ds(pl.multiple_of(g * HEAD_DIM, HEAD_DIM), HEAD_DIM)
        queries = jnp.concatenate(
            [
                q_ref[:, pl.ds(pl.multiple_of((g * group + i) * HEAD_DIM, HEAD_DIM), HEAD_DIM)]
                for i in range(group)
            ],
            axis=0,
        )
        keys = jnp.concatenate([k0_ref[:, lanes], k2_ref[:, lanes], k1_ref[:, lanes]], axis=0)
        dots = lax.dot_general(
            keys, queries, (((1,), (1,)), ((), ())), preferred_element_type=f32
        )
        slopes = []
        for i in range(group):
            mine = dots[:, i * rows : (i + 1) * rows]
            score = (
                jnp.concatenate(
                    [jnp.where(near, mine[:rows], mine[rows : 2 * rows]), mine[2 * rows :]], axis=0
                )
                * scaling
            )
            held = jnp.where(allowed, score, negative)
            peak = jnp.max(held, axis=0, keepdims=True)
            raised = jnp.exp(held - peak)
            total = jnp.sum(raised, axis=0, keepdims=True)
            weight = raised * (1.0 / total)
            labels = pl.ds(pl.multiple_of((g * group + i) * top, top), top)
            spot_rows, prob_rows = spot_scr[labels, :], prob_scr[labels, :]
            table = jnp.zeros((window, rows), f32)
            for k in range(top):
                table = table + jnp.where(
                    spots == spot_rows[k : k + 1], prob_rows[k : k + 1], 0.0
                )
            mass = jnp.sum(prob_rows, axis=0, keepdims=True)
            loss = loss + mass * (peak + jnp.log(total))
            loss = loss - jnp.sum(table * score, axis=0, keepdims=True)
            weight_ref[g, :, i * rows : (i + 1) * rows] = parted(weight)
            slopes.append(parted((weight * mass - table) * (1.0 / heads)))
        grads = jnp.dot(
            jnp.concatenate(slopes, axis=1), queries, preferred_element_type=f32
        ) * scaling
        g0_ref[:, lanes] = grads[:rows]
        g2_ref[:, lanes] = grads[rows : 2 * rows].astype(bf16)
        g1_ref[:, lanes] = grads[2 * rows :].astype(bf16)
        return loss

    loss = lax.fori_loop(0, kv_count, one_group, entropy)
    loss_ref[...] = loss * (1.0 / heads)


def output_kernel(weight_ref, v0_ref, v1_ref, v2_ref, out_ref):
    bf16, f32 = jnp.bfloat16, jnp.float32
    rows = v0_ref.shape[0]
    group = weight_ref.shape[2] // rows
    for g in range(weight_ref.shape[0]):
        lanes = slice(g * HEAD_DIM, (g + 1) * HEAD_DIM)
        values = jnp.concatenate([v0_ref[:, lanes], v2_ref[:, lanes], v1_ref[:, lanes]], axis=0)
        flipped = jnp.dot(
            values.astype(f32).T.astype(bf16), weight_ref[g], preferred_element_type=f32
        )
        for i in range(group):
            h = g * group + i
            out_ref[:, h * HEAD_DIM : (h + 1) * HEAD_DIM] = (
                flipped[:, i * rows : (i + 1) * rows].T.astype(bf16)
            )


def attend(start, queries, keys, pick, prob):
    rows, kv_width = keys[0].shape
    kv_count = kv_width // HEAD_DIM
    group = queries.shape[1] // kv_width
    bf16, f32 = jnp.bfloat16, jnp.float32
    struct = jax.ShapeDtypeStruct
    return pl.pallas_call(
        attend_kernel,
        out_shape=[
            struct((rows, kv_width), f32),
            struct((rows, kv_width), bf16),
            struct((rows, kv_width), bf16),
            struct((1, rows), f32),
            struct((kv_count, (SPAN + 1) * rows, group * rows), bf16),
        ],
        in_specs=whole(7),
        out_specs=whole(5),
        scratch_shapes=[pltpu.VMEM(pick.shape[::-1], f32)] * 2,
        compiler_params=GRANT,
        name="attend",
    )(start.reshape(1, rows), queries, *keys, pick, prob)


def attend_output(weights, values):
    rows = values[0].shape[0]
    heads = weights.shape[0] * weights.shape[2] // rows
    return pl.pallas_call(
        output_kernel,
        out_shape=jax.ShapeDtypeStruct((rows, heads * HEAD_DIM), jnp.bfloat16),
        in_specs=whole(4),
        out_specs=whole()[0],
        compiler_params=GRANT,
        name="attend_output",
    )(weights, *values)


def whole(count=1):
    return [pl.BlockSpec(memory_space=pltpu.VMEM)] * count


def pack_rows(hidden, queries, values, row_target, seq_count):
    rows = hidden.shape[0]
    tiles = (hidden.shape[1] + queries.shape[1] + values.shape[1]) // HEAD_DIM
    main = tiles - tiles // 4
    return pl.pallas_call(
        pack_kernel,
        out_shape=jax.ShapeDtypeStruct((seq_count * 8, (main + 1) * HEAD_DIM), jnp.bfloat16),
        in_specs=whole(4),
        out_specs=whole()[0],
        compiler_params=GRANT,
        name="pack_rows",
    )(row_target.reshape(1, rows), hidden, queries, values)


def unpack_hidden(got, place_of, rows, width):
    return pl.pallas_call(
        hidden_kernel,
        out_shape=[jax.ShapeDtypeStruct((rows, width // 2), jnp.bfloat16)] * 4,
        in_specs=[pl.BlockSpec(memory_space=pltpu.SMEM)] + whole(),
        out_specs=whole(4),
        compiler_params=GRANT,
        name="unpack_hidden",
    )(place_of, got)


def unpack_rest(got, rows, width, kv_width):
    return pl.pallas_call(
        rest_kernel,
        out_shape=[jax.ShapeDtypeStruct((rows, w), jnp.bfloat16) for w in (width, kv_width)],
        in_specs=whole(),
        out_specs=whole(2),
        compiler_params=GRANT,
        name="unpack_rest",
    )(got)


def local(
    hidden, queries, values, row_target, key_weight, dialogue_lengths, teacher_pick, teacher_prob
):
    bf16, f32 = jnp.bfloat16, jnp.float32
    local_rows, width = hidden.shape
    seq_count = lax.axis_size(SEQ)
    seq_index = lax.axis_index(SEQ)
    lines = lax.axis_size("y")
    device_count = seq_count * lines * lax.axis_size("core")
    kv_width = values.shape[1]

    place_of = jnp.stack([lax.axis_index("core"), lax.axis_index("y")]).astype(jnp.int32)

    plane_rows = exchange(jnp.broadcast_to(key_weight, (seq_count,) + key_weight.shape), SEQ)
    plane_rows = plane_rows.reshape(local_rows, kv_width)
    own_half = jnp.concatenate(
        [plane_rows] + [line_shift(plane_rows, by) for by in range(1, lines)], axis=0
    )
    other_half = core_swap(own_half)

    parcels = pack_rows(hidden, queries, values, row_target, seq_count)
    received = exchange(parcels.reshape(seq_count, 8, -1), SEQ)
    got = received.reshape(seq_count * 8, -1)
    mine, theirs, mine_turned, theirs_turned = unpack_hidden(got, place_of, local_rows, width)
    queries_seq, values_seq = unpack_rest(got, local_rows, width, kv_width)

    positions = seq_index * local_rows + jnp.arange(local_rows, dtype=jnp.int32)
    cosine, sine = turn_angles(positions)
    keys_seq = rotate(
        jnp.dot(mine_turned, own_half, preferred_element_type=f32)
        + jnp.dot(theirs_turned, other_half, preferred_element_type=f32),
        cosine,
        sine,
    ).astype(bf16)
    starts = dialogue_starts(dialogue_lengths[0], positions)
    keys = [keys_seq] + [seq_shift(keys_seq, by) for by in range(1, SPAN + 1)]
    own_grad, grad_1, grad_2, token_loss, weights = attend(
        starts - seq_index * local_rows, queries_seq, keys, teacher_pick, teacher_prob
    )
    values_late, own_grad = lax.optimization_barrier((values_seq, own_grad))
    back_1, back_2, values_1, values_2 = lax.optimization_barrier(
        (
            seq_shift(grad_1, -1),
            seq_shift(grad_2, -2),
            seq_shift(values_late, 1),
            seq_shift(values_late, 2),
        )
    )
    attn_out = attend_output(weights, (values_seq, values_1, values_2))
    rotated_grad = own_grad + back_1.astype(f32) + back_2.astype(f32)
    key_grad = rotate(rotated_grad, cosine, -sine).astype(bf16)

    inverse_root = (local_rows * device_count) ** (-0.5)
    def term(tiles_of):
        return jnp.einsum(
            "td,tc->dc", tiles_of, key_grad, preferred_element_type=f32
        )

    from_other = core_swap(term(theirs).astype(bf16))
    summed = (term(mine) + from_other.astype(f32)).astype(bf16)
    half = lines // 2
    pieces = jnp.transpose(
        summed.reshape(2, half, seq_count // 2, 8, kv_width), (2, 0, 3, 1, 4)
    ).reshape(seq_count, 8, half * kv_width)
    plane = jnp.sum(exchange(pieces, SEQ).astype(f32), axis=0)
    plane = jnp.transpose(plane.reshape(2, 4, half, kv_width), (2, 0, 1, 3))
    side = lax.axis_index("xl")
    empty = jnp.zeros_like(plane)
    last = jnp.stack([jnp.where(side == 0, plane, empty), jnp.where(side == 1, plane, empty)])
    weight_grad = jnp.sum(
        exchange(last.reshape(2 * lines, 4, kv_width), ("y", "xl")), axis=0
    ) * inverse_root
    return (attn_out, token_loss.reshape(local_rows), weight_grad)


def solution(mesh):
    fine = Mesh(np.asarray(mesh.devices).reshape(8, 2, 8, 2, 2), EVERY)
    pack = ("y", "core")
    placed = (
        P(EVERY, None),
        P(EVERY, None),
        P(EVERY, None),
        P(EVERY),
        P(EVERY, None),
        P(pack, None),
        P(EVERY, None),
        P(EVERY, None),
    )
    return jax.shard_map(
        local,
        mesh=fine,
        in_specs=placed,
        out_specs=(P(EVERY, None), P(EVERY), P(EVERY, None)),
        check_vma=False,
    )
```

```python
import functools

import jax
import jax.numpy as jnp
import numpy as np
from jax import lax
from jax.experimental import pallas as pl
from jax.experimental.pallas import tpu as pltpu
from jax.sharding import Mesh
from jax.sharding import PartitionSpec as P

HEAD_DIM = 128
SPAN = 2
SLOTS = 6

negative = -1e30
rope_base = 500000.0

GRANT = pltpu.CompilerParams(vmem_limit_bytes=24 << 20)

ACROSS = ("xh", "xl")
SEQ = ("z",) + ACROSS
EVERY = ("y", "core") + SEQ


def exchange(pieces, axes):
    return lax.all_to_all(pieces, axes, split_axis=0, concat_axis=0, tiled=True)


def seq_shift(shard, by):
    devices = lax.axis_size(SEQ)
    pairs = [(i, i + by) for i in range(devices) if 0 <= i + by < devices]
    return lax.ppermute(shard, SEQ, pairs)


def line_shift(shard, by):
    devices = lax.axis_size("y")
    return lax.ppermute(shard, "y", [(i, (i + by) % devices) for i in range(devices)])


def core_swap(shard):
    return lax.ppermute(shard, "core", [(0, 1), (1, 0)])


def turn_angles(positions):
    halfway = HEAD_DIM // 2
    frequency = rope_base ** (-2.0 * jnp.arange(halfway, dtype=jnp.float32) / HEAD_DIM)
    angle = positions.astype(jnp.float32)[:, None] * frequency[None, :]
    return jnp.cos(angle)[:, None, :], jnp.sin(angle)[:, None, :]


def rotate(matrix, cosine, sine):
    count = matrix.shape[0]
    halfway = HEAD_DIM // 2
    split = matrix.reshape(count, -1, HEAD_DIM)
    first_half = split[..., :halfway]
    second_half = split[..., halfway:]
    joined = jnp.concatenate(
        [first_half * cosine - second_half * sine, second_half * cosine + first_half * sine],
        axis=-1,
    )
    return joined.reshape(count, -1)


def dialogue_starts(lengths, positions):
    ending = jnp.cumsum(lengths)
    picked = jnp.where(ending[None, :] <= positions[:, None], lengths[None, :], 0)
    return jnp.sum(picked, axis=1)


def pack_kernel(target_ref, hidden_ref, queries_ref, values_ref, out_ref):
    bf16, f32 = jnp.bfloat16, jnp.float32
    rows = hidden_ref.shape[0]
    parcels = out_ref.shape[0]
    main = out_ref.shape[1] // HEAD_DIM - 1
    third = main // 3
    refs = (hidden_ref, queries_ref, values_ref)
    tiles = [ref[:, i * HEAD_DIM : (i + 1) * HEAD_DIM] for ref in refs for i in range(ref.shape[1] // HEAD_DIM)]
    target = target_ref[...]
    block = target // rows
    offset = (target - block * rows - rows).astype(f32)
    across = jnp.broadcast_to(block.astype(f32), (rows, rows))
    down = across.T
    first = lax.broadcasted_iota(jnp.int32, (rows, rows), 0)
    second = lax.broadcasted_iota(jnp.int32, (rows, rows), 1)
    rank = jnp.sum(jnp.where((across == down) & (first < second), 1.0, 0.0), axis=0, keepdims=True)
    rank = rank.astype(jnp.int32)
    row = lax.broadcasted_iota(jnp.int32, (parcels, rows), 0)
    place = row % 8
    to_block = block == row // 8
    low = jnp.where(to_block & (place == rank) & (place < SLOTS), 1.0, 0.0)
    lane = lax.broadcasted_iota(jnp.int32, (parcels, HEAD_DIM), 1)
    meta = jnp.zeros((parcels, HEAD_DIM), f32)
    extras = jnp.concatenate(tiles[main:], axis=1)
    for m in range(3):
        high = jnp.where(
            to_block & (place - SLOTS + 2 * m == rank) & (place >= SLOTS), 1.0, 0.0
        )
        place_of = jnp.sum((low + high) * offset, axis=1, keepdims=True) + rows
        meta = jnp.where(lane == m, place_of, meta)
        select = jnp.concatenate([low, high], axis=1).astype(bf16)
        both = jnp.concatenate([jnp.concatenate(tiles[m:main:3], axis=1), extras], axis=0)
        done = jnp.dot(select, both, preferred_element_type=f32).astype(bf16)
        for i in range(third):
            g = 3 * i + m
            out_ref[:, g * HEAD_DIM : (g + 1) * HEAD_DIM] = done[:, i * HEAD_DIM : (i + 1) * HEAD_DIM]
    out_ref[:, main * HEAD_DIM :] = meta.astype(bf16)


def tile_columns(ref, indices):
    return jnp.concatenate([ref[:, g * HEAD_DIM : (g + 1) * HEAD_DIM] for g in indices], axis=1)


def arrivals(got_ref, rows):
    parcels = got_ref.shape[0]
    main = got_ref.shape[1] // HEAD_DIM - 1
    meta = got_ref[:, main * HEAD_DIM :].astype(jnp.float32).T
    token = lax.broadcasted_iota(jnp.int32, (rows, parcels), 0).astype(jnp.float32)
    low = lax.broadcasted_iota(jnp.int32, (rows, parcels), 1) % 8 < SLOTS
    hits = [meta[m : m + 1, :] == token for m in range(3)]
    into = jnp.where(hits[0] & low, 1.0, 0.0).astype(jnp.bfloat16)
    late = [jnp.where(hit & ~low, 1.0, 0.0).astype(jnp.bfloat16) for hit in hits]
    return main, into, late


def project_kernel(
    sides, place_ref, got_ref, own_ref, other_ref, cosine_ref, sine_ref,
    keys_ref, mine_ref, theirs_ref, mine_turned, theirs_turned,
):
    bf16, f32 = jnp.bfloat16, jnp.float32
    rows = mine_ref.shape[0]
    count = mine_ref.shape[1] // HEAD_DIM
    _, into, _ = arrivals(got_ref, rows)
    done = jnp.dot(into, got_ref[:, : 2 * count * HEAD_DIM], preferred_element_type=f32)
    is_first = jnp.broadcast_to(place_ref[0], (rows, HEAD_DIM)) == 0
    own_tiles, other_tiles = [], []
    for i in range(count):
        even = done[:, 2 * i * HEAD_DIM : (2 * i + 1) * HEAD_DIM]
        odd = done[:, (2 * i + 1) * HEAD_DIM : (2 * i + 2) * HEAD_DIM]
        own = jnp.where(is_first, even, odd).astype(bf16)
        other = jnp.where(is_first, odd, even).astype(bf16)
        own_tiles.append(own)
        other_tiles.append(other)
        turned = lax.rem(place_ref[1] - i + count, count)
        lanes = pl.ds(pl.multiple_of(turned * HEAD_DIM, HEAD_DIM), HEAD_DIM)
        mine_turned[:, lanes] = own
        theirs_turned[:, lanes] = other
    keys = jnp.dot(mine_turned[...], own_ref[...], preferred_element_type=f32)
    keys = keys + jnp.dot(theirs_turned[...], other_ref[...], preferred_element_type=f32)
    for h in range(keys.shape[1] // HEAD_DIM):
        head = keys[:, h * HEAD_DIM : (h + 1) * HEAD_DIM]
        swapped = pltpu.roll(head, HEAD_DIM // 2, 1)
        keys_ref[:, h * HEAD_DIM : (h + 1) * HEAD_DIM] = (
            head * cosine_ref[...] + swapped * sine_ref[...]
        ).astype(bf16)
    source = lax.broadcasted_iota(jnp.int32, (HEAD_DIM, HEAD_DIM), 0)
    target = lax.broadcasted_iota(jnp.int32, (HEAD_DIM, HEAD_DIM), 1)
    part = HEAD_DIM // sides
    wanted = (target % part) // 4 * (4 * sides) + target // part * 4 + target % 4
    order = jnp.where(source == wanted, 1.0, 0.0).astype(bf16)
    for tiles, ref in ((own_tiles, mine_ref), (other_tiles, theirs_ref)):
        moved = jnp.dot(
            jnp.concatenate(tiles, axis=0), order, preferred_element_type=f32
        ).astype(bf16)
        for i in range(count):
            ref[:, i * HEAD_DIM : (i + 1) * HEAD_DIM] = moved[i * rows : (i + 1) * rows]


def rest_kernel(got_ref, queries_ref, values_ref):
    bf16, f32 = jnp.bfloat16, jnp.float32
    rows, width = queries_ref.shape
    main, into, late = arrivals(got_ref, rows)
    first = jnp.dot(into, got_ref[:, width : main * HEAD_DIM], preferred_element_type=f32)
    first_width = first.shape[1]
    queries_ref[:, :first_width] = first.astype(bf16)
    extras = jnp.zeros((rows, main // 3 * HEAD_DIM), f32)
    for m in range(3):
        extras = extras + jnp.dot(
            late[m], tile_columns(got_ref, range(m, main, 3)), preferred_element_type=f32
        )
    extras = extras.astype(bf16)
    queries_ref[:, first_width:] = extras[:, : width - first_width]
    values_ref[...] = extras[:, width - first_width :]


def attend_kernel(
    start_ref, q_ref, k0_ref, k1_ref, k2_ref, pick_ref, prob_ref,
    g0_ref, g1_ref, g2_ref, loss_ref, weight_ref, spot_scr, prob_scr,
):
    bf16, f32 = jnp.bfloat16, jnp.float32
    rows = q_ref.shape[0]
    kv_count = k0_ref.shape[1] // HEAD_DIM
    heads = q_ref.shape[1] // HEAD_DIM
    group = heads // kv_count
    top = pick_ref.shape[1] // heads
    window = SPAN * rows
    scaling = HEAD_DIM ** (-0.5)
    query = lax.broadcasted_iota(jnp.int32, (1, rows), 1).astype(f32)
    start = start_ref[...].astype(f32)
    reach = query - start + 1.0
    picked = pick_ref[...].astype(f32).T
    rest = picked - jnp.floor(picked / reach) * reach
    rest = jnp.where(rest < 0.0, rest + reach, rest)
    rest = jnp.where(rest >= reach, rest - reach, rest)
    spot = start + rest
    spot_scr[...] = jnp.where(spot < 0.0, spot + window, spot)
    prob_all = prob_ref[...].T
    prob_scr[...] = prob_all
    entropy = jnp.sum(prob_all * jnp.log(prob_all), axis=0, keepdims=True)
    spots = lax.broadcasted_iota(jnp.int32, (window, rows), 0).astype(f32)
    across = lax.broadcasted_iota(jnp.int32, (window, rows), 1).astype(f32)
    position = jnp.where(spots <= across, spots, spots - window)
    allowed = position >= start
    near = spots[:rows] <= across[:rows]

    def parted(rows_of):
        low = rows_of[:rows]
        return jnp.concatenate(
            [jnp.where(near, low, 0.0), jnp.where(near, 0.0, low), rows_of[rows:]], axis=0
        ).astype(bf16)

    def one_group(g, loss):
        lanes = pl.ds(pl.multiple_of(g * HEAD_DIM, HEAD_DIM), HEAD_DIM)
        queries = jnp.concatenate(
            [
                q_ref[:, pl.ds(pl.multiple_of((g * group + i) * HEAD_DIM, HEAD_DIM), HEAD_DIM)]
                for i in range(group)
            ],
            axis=0,
        )
        keys = jnp.concatenate([k0_ref[:, lanes], k2_ref[:, lanes], k1_ref[:, lanes]], axis=0)
        dots = lax.dot_general(
            keys, queries, (((1,), (1,)), ((), ())), preferred_element_type=f32
        )
        slopes = []
        for i in range(group):
            mine = dots[:, i * rows : (i + 1) * rows]
            score = (
                jnp.concatenate(
                    [jnp.where(near, mine[:rows], mine[rows : 2 * rows]), mine[2 * rows :]], axis=0
                )
                * scaling
            )
            held = jnp.where(allowed, score, negative)
            peak = jnp.max(held, axis=0, keepdims=True)
            raised = jnp.exp(held - peak)
            total = jnp.sum(raised, axis=0, keepdims=True)
            weight = raised * (1.0 / total)
            labels = pl.ds(pl.multiple_of((g * group + i) * top, top), top)
            spot_rows, prob_rows = spot_scr[labels, :], prob_scr[labels, :]
            table = jnp.zeros((window, rows), f32)
            for k in range(top):
                table = table + jnp.where(
                    spots == spot_rows[k : k + 1], prob_rows[k : k + 1], 0.0
                )
            mass = jnp.sum(prob_rows, axis=0, keepdims=True)
            loss = loss + mass * (peak + jnp.log(total))
            loss = loss - jnp.sum(table * score, axis=0, keepdims=True)
            weight_ref[g, :, i * rows : (i + 1) * rows] = parted(weight)
            slopes.append(parted((weight * mass - table) * (1.0 / heads)))
        grads = jnp.dot(
            jnp.concatenate(slopes, axis=1), queries, preferred_element_type=f32
        ) * scaling
        g0_ref[:, lanes] = grads[:rows]
        g2_ref[:, lanes] = grads[rows : 2 * rows].astype(bf16)
        g1_ref[:, lanes] = grads[2 * rows :].astype(bf16)
        return loss

    loss = lax.fori_loop(0, kv_count, one_group, entropy)
    loss_ref[...] = loss * (1.0 / heads)


def output_kernel(weight_ref, v0_ref, v1_ref, v2_ref, out_ref):
    bf16, f32 = jnp.bfloat16, jnp.float32
    rows = v0_ref.shape[0]
    group = weight_ref.shape[2] // rows
    for g in range(weight_ref.shape[0]):
        lanes = slice(g * HEAD_DIM, (g + 1) * HEAD_DIM)
        values = jnp.concatenate([v0_ref[:, lanes], v2_ref[:, lanes], v1_ref[:, lanes]], axis=0)
        flipped = jnp.dot(
            values.astype(f32).T.astype(bf16), weight_ref[g], preferred_element_type=f32
        )
        for i in range(group):
            h = g * group + i
            out_ref[:, h * HEAD_DIM : (h + 1) * HEAD_DIM] = (
                flipped[:, i * rows : (i + 1) * rows].T.astype(bf16)
            )


def attend(start, queries, keys, pick, prob):
    rows, kv_width = keys[0].shape
    kv_count = kv_width // HEAD_DIM
    group = queries.shape[1] // kv_width
    bf16, f32 = jnp.bfloat16, jnp.float32
    struct = jax.ShapeDtypeStruct
    return pl.pallas_call(
        attend_kernel,
        out_shape=[
            struct((rows, kv_width), f32),
            struct((rows, kv_width), bf16),
            struct((rows, kv_width), bf16),
            struct((1, rows), f32),
            struct((kv_count, (SPAN + 1) * rows, group * rows), bf16),
        ],
        in_specs=whole(7),
        out_specs=whole(5),
        scratch_shapes=[pltpu.VMEM(pick.shape[::-1], f32)] * 2,
        compiler_params=GRANT,
        name="attend",
    )(start.reshape(1, rows), queries, *keys, pick, prob)


def attend_output(weights, values):
    rows = values[0].shape[0]
    heads = weights.shape[0] * weights.shape[2] // rows
    return pl.pallas_call(
        output_kernel,
        out_shape=jax.ShapeDtypeStruct((rows, heads * HEAD_DIM), jnp.bfloat16),
        in_specs=whole(4),
        out_specs=whole()[0],
        compiler_params=GRANT,
        name="attend_output",
    )(weights, *values)


def whole(count=1):
    return [pl.BlockSpec(memory_space=pltpu.VMEM)] * count


def pack_rows(hidden, queries, values, row_target, seq_count):
    rows = hidden.shape[0]
    tiles = (hidden.shape[1] + queries.shape[1] + values.shape[1]) // HEAD_DIM
    main = tiles - tiles // 4
    return pl.pallas_call(
        pack_kernel,
        out_shape=jax.ShapeDtypeStruct((seq_count * 8, (main + 1) * HEAD_DIM), jnp.bfloat16),
        in_specs=whole(4),
        out_specs=whole()[0],
        compiler_params=GRANT,
        name="pack_rows",
    )(row_target.reshape(1, rows), hidden, queries, values)


def project(got, place_of, own_half, other_half, cosine, sine, sides):
    rows, (width, kv_width) = cosine.shape[0], own_half.shape
    struct = jax.ShapeDtypeStruct
    return pl.pallas_call(
        functools.partial(project_kernel, sides),
        out_shape=[struct((rows, w), jnp.bfloat16) for w in (kv_width, width, width)],
        in_specs=[pl.BlockSpec(memory_space=pltpu.SMEM)] + whole(5),
        out_specs=whole(3),
        scratch_shapes=[pltpu.VMEM((rows, width), jnp.bfloat16)] * 2,
        compiler_params=GRANT,
        name="project",
    )(place_of, got, own_half, other_half, cosine, sine)


def unpack_rest(got, rows, width, kv_width):
    return pl.pallas_call(
        rest_kernel,
        out_shape=[jax.ShapeDtypeStruct((rows, w), jnp.bfloat16) for w in (width, kv_width)],
        in_specs=whole(),
        out_specs=whole(2),
        compiler_params=GRANT,
        name="unpack_rest",
    )(got)


def local(
    hidden, queries, values, row_target, key_weight, dialogue_lengths, teacher_pick, teacher_prob
):
    bf16, f32 = jnp.bfloat16, jnp.float32
    local_rows, width = hidden.shape
    seq_count = lax.axis_size(SEQ)
    seq_index = lax.axis_index(SEQ)
    lines = lax.axis_size("y")
    device_count = seq_count * lines * lax.axis_size("core")
    kv_width = values.shape[1]

    place_of = jnp.stack([lax.axis_index("core"), lax.axis_index("y")]).astype(jnp.int32)

    plane_rows = exchange(jnp.broadcast_to(key_weight, (seq_count,) + key_weight.shape), SEQ)
    plane_rows = plane_rows.reshape(local_rows, kv_width)
    own_half = jnp.concatenate(
        [plane_rows] + [line_shift(plane_rows, by) for by in range(1, lines)], axis=0
    )
    other_half = core_swap(own_half)

    parcels = pack_rows(hidden, queries, values, row_target, seq_count)
    received = exchange(parcels.reshape(seq_count, 8, -1), SEQ)
    got = received.reshape(seq_count * 8, -1)
    positions = seq_index * local_rows + jnp.arange(local_rows, dtype=jnp.int32)
    cosine, sine = turn_angles(positions)
    keys_seq, mine, theirs = project(
        got,
        place_of,
        own_half,
        other_half,
        jnp.concatenate([cosine[:, 0], cosine[:, 0]], axis=1),
        jnp.concatenate([-sine[:, 0], sine[:, 0]], axis=1),
        lax.axis_size(ACROSS),
    )
    queries_seq, values_seq = unpack_rest(got, local_rows, width, kv_width)

    starts = dialogue_starts(dialogue_lengths[0], positions)
    keys = [keys_seq] + [seq_shift(keys_seq, by) for by in range(1, SPAN + 1)]
    own_grad, grad_1, grad_2, token_loss, weights = attend(
        starts - seq_index * local_rows, queries_seq, keys, teacher_pick, teacher_prob
    )
    rotated_grad = (
        own_grad + seq_shift(grad_1, -1).astype(f32) + seq_shift(grad_2, -2).astype(f32)
    )
    key_grad = rotate(rotated_grad, cosine, -sine).astype(bf16)

    inverse_root = (local_rows * device_count) ** (-0.5)
    def term(tiles_of):
        return jnp.einsum(
            "td,tc->dc", tiles_of, key_grad, preferred_element_type=f32
        )

    from_other = core_swap(term(theirs).astype(bf16))
    summed = (term(mine) + from_other.astype(f32)).astype(bf16)
    sides = lax.axis_size(ACROSS)
    pieces = jnp.transpose(summed.reshape(lines, sides, -1, kv_width), (1, 0, 2, 3))
    values_late, pieces = lax.optimization_barrier(
        (values_seq, pieces.reshape(sides, -1, kv_width))
    )
    line = jnp.sum(exchange(pieces, ACROSS).astype(f32), axis=0).astype(bf16)
    values_all = [values_seq] + [seq_shift(values_late, by) for by in range(1, SPAN + 1)]
    attn_out = attend_output(weights, values_all)
    last = exchange(line.reshape(-1, 4, kv_width), ("y", "z"))
    weight_grad = jnp.sum(last.astype(f32), axis=0) * inverse_root
    return (attn_out, token_loss.reshape(local_rows), weight_grad)


def solution(mesh):
    fine = Mesh(np.asarray(mesh.devices).reshape(8, 2, 8, 2, 2), EVERY)
    pack = ("y", "core")
    placed = (
        P(EVERY, None),
        P(EVERY, None),
        P(EVERY, None),
        P(EVERY),
        P(EVERY, None),
        P(pack, None),
        P(EVERY, None),
        P(EVERY, None),
    )
    return jax.shard_map(
        local,
        mesh=fine,
        in_specs=placed,
        out_specs=(P(EVERY, None), P(EVERY), P(EVERY, None)),
        check_vma=False,
    )
```

```python
import functools

import jax
import jax.numpy as jnp
import numpy as np
from jax import lax
from jax.experimental import pallas as pl
from jax.experimental.pallas import tpu as pltpu
from jax.sharding import Mesh
from jax.sharding import PartitionSpec as P


HEAD_DIM = 128
SPAN = 2
SLOTS = 6

negative = -1e30
rope_base = 500000.0

GRANT = pltpu.CompilerParams(vmem_limit_bytes=24 << 20)

ACROSS = ("xh", "xl")
SEQ = ("z",) + ACROSS
EVERY = ("y", "core") + SEQ


def exchange(pieces, axes):
    return lax.all_to_all(pieces, axes, split_axis=0, concat_axis=0, tiled=True)


def seq_shift(shard, by):
    devices = lax.axis_size(SEQ)
    pairs = [(i, i + by) for i in range(devices) if 0 <= i + by < devices]
    return lax.ppermute(shard, SEQ, pairs)


def line_shift(shard, by):
    devices = lax.axis_size("y")
    return lax.ppermute(shard, "y", [(i, (i + by) % devices) for i in range(devices)])


def core_swap(shard):
    return lax.ppermute(shard, "core", [(0, 1), (1, 0)])


def turn_angles(positions):
    halfway = HEAD_DIM // 2
    frequency = rope_base ** (-2.0 * jnp.arange(halfway, dtype=jnp.float32) / HEAD_DIM)
    angle = positions.astype(jnp.float32)[:, None] * frequency[None, :]
    return jnp.cos(angle)[:, None, :], jnp.sin(angle)[:, None, :]


def rotate(matrix, cosine, sine):
    count = matrix.shape[0]
    halfway = HEAD_DIM // 2
    split = matrix.reshape(count, -1, HEAD_DIM)
    first_half = split[..., :halfway]
    second_half = split[..., halfway:]
    joined = jnp.concatenate(
        [first_half * cosine - second_half * sine, second_half * cosine + first_half * sine],
        axis=-1,
    )
    return joined.reshape(count, -1)


def dialogue_starts(lengths, positions):
    ending = jnp.cumsum(lengths)
    picked = jnp.where(ending[None, :] <= positions[:, None], lengths[None, :], 0)
    return jnp.sum(picked, axis=1)


def pack_kernel(target_ref, hidden_ref, queries_ref, values_ref, out_ref):
    bf16, f32 = jnp.bfloat16, jnp.float32
    rows = hidden_ref.shape[0]
    parcels = out_ref.shape[0]
    main = out_ref.shape[1] // HEAD_DIM - 1
    third = main // 3
    refs = (hidden_ref, queries_ref, values_ref)
    tiles = [ref[:, i * HEAD_DIM : (i + 1) * HEAD_DIM] for ref in refs for i in range(ref.shape[1] // HEAD_DIM)]
    target = target_ref[...]
    block = target // rows
    offset = (target - block * rows - rows).astype(f32)
    across = jnp.broadcast_to(block.astype(f32), (rows, rows))
    down = across.T
    first = lax.broadcasted_iota(jnp.int32, (rows, rows), 0)
    second = lax.broadcasted_iota(jnp.int32, (rows, rows), 1)
    rank = jnp.sum(jnp.where((across == down) & (first < second), 1.0, 0.0), axis=0, keepdims=True)
    rank = rank.astype(jnp.int32)
    row = lax.broadcasted_iota(jnp.int32, (parcels, rows), 0)
    place = row % 8
    to_block = block == row // 8
    low = jnp.where(to_block & (place == rank) & (place < SLOTS), 1.0, 0.0)
    lane = lax.broadcasted_iota(jnp.int32, (parcels, HEAD_DIM), 1)
    meta = jnp.zeros((parcels, HEAD_DIM), f32)
    extras = jnp.concatenate(tiles[main:], axis=1)
    for m in range(3):
        high = jnp.where(
            to_block & (place - SLOTS + 2 * m == rank) & (place >= SLOTS), 1.0, 0.0
        )
        place_of = jnp.sum((low + high) * offset, axis=1, keepdims=True) + rows
        meta = jnp.where(lane == m, place_of, meta)
        select = jnp.concatenate([low, high], axis=1).astype(bf16)
        both = jnp.concatenate([jnp.concatenate(tiles[m:main:3], axis=1), extras], axis=0)
        done = jnp.dot(select, both, preferred_element_type=f32).astype(bf16)
        for i in range(third):
            g = 3 * i + m
            out_ref[:, g * HEAD_DIM : (g + 1) * HEAD_DIM] = done[:, i * HEAD_DIM : (i + 1) * HEAD_DIM]
    out_ref[:, main * HEAD_DIM :] = meta.astype(bf16)


def tile_columns(ref, indices):
    return jnp.concatenate([ref[:, g * HEAD_DIM : (g + 1) * HEAD_DIM] for g in indices], axis=1)


def arrivals(got_ref, rows):
    parcels = got_ref.shape[0]
    main = got_ref.shape[1] // HEAD_DIM - 1
    meta = got_ref[:, main * HEAD_DIM :].astype(jnp.float32).T
    token = lax.broadcasted_iota(jnp.int32, (rows, parcels), 0).astype(jnp.float32)
    low = lax.broadcasted_iota(jnp.int32, (rows, parcels), 1) % 8 < SLOTS
    hits = [meta[m : m + 1, :] == token for m in range(3)]
    into = jnp.where(hits[0] & low, 1.0, 0.0).astype(jnp.bfloat16)
    late = [jnp.where(hit & ~low, 1.0, 0.0).astype(jnp.bfloat16) for hit in hits]
    return main, into, late


def project_kernel(
    sides, place_ref, got_ref, own_ref, other_ref, cosine_ref, sine_ref,
    keys_ref, mine_ref, theirs_ref, mine_turned, theirs_turned,
):
    bf16, f32 = jnp.bfloat16, jnp.float32
    rows = mine_ref.shape[0]
    count = mine_ref.shape[1] // HEAD_DIM
    _, into, _ = arrivals(got_ref, rows)
    done = jnp.dot(into, got_ref[:, : 2 * count * HEAD_DIM], preferred_element_type=f32)
    is_first = jnp.broadcast_to(place_ref[0], (rows, HEAD_DIM)) == 0
    own_tiles, other_tiles = [], []
    for i in range(count):
        even = done[:, 2 * i * HEAD_DIM : (2 * i + 1) * HEAD_DIM]
        odd = done[:, (2 * i + 1) * HEAD_DIM : (2 * i + 2) * HEAD_DIM]
        own = jnp.where(is_first, even, odd).astype(bf16)
        other = jnp.where(is_first, odd, even).astype(bf16)
        own_tiles.append(own)
        other_tiles.append(other)
        turned = lax.rem(place_ref[1] - i + count, count)
        lanes = pl.ds(pl.multiple_of(turned * HEAD_DIM, HEAD_DIM), HEAD_DIM)
        mine_turned[:, lanes] = own
        theirs_turned[:, lanes] = other
    keys = jnp.dot(mine_turned[...], own_ref[...], preferred_element_type=f32)
    keys = keys + jnp.dot(theirs_turned[...], other_ref[...], preferred_element_type=f32)
    for h in range(keys.shape[1] // HEAD_DIM):
        head = keys[:, h * HEAD_DIM : (h + 1) * HEAD_DIM]
        swapped = pltpu.roll(head, HEAD_DIM // 2, 1)
        keys_ref[:, h * HEAD_DIM : (h + 1) * HEAD_DIM] = (
            head * cosine_ref[...] + swapped * sine_ref[...]
        ).astype(bf16)
    source = lax.broadcasted_iota(jnp.int32, (HEAD_DIM, HEAD_DIM), 0)
    target = lax.broadcasted_iota(jnp.int32, (HEAD_DIM, HEAD_DIM), 1)
    part = HEAD_DIM // sides
    wanted = (target % part) // 4 * (4 * sides) + target // part * 4 + target % 4
    order = jnp.where(source == wanted, 1.0, 0.0).astype(bf16)
    for tiles, ref in ((own_tiles, mine_ref), (other_tiles, theirs_ref)):
        moved = jnp.dot(
            jnp.concatenate(tiles, axis=0), order, preferred_element_type=f32
        ).astype(bf16)
        for i in range(count):
            ref[:, i * HEAD_DIM : (i + 1) * HEAD_DIM] = moved[i * rows : (i + 1) * rows]


def rest_kernel(got_ref, queries_ref, values_ref):
    bf16, f32 = jnp.bfloat16, jnp.float32
    rows, width = queries_ref.shape
    main, into, late = arrivals(got_ref, rows)
    first = jnp.dot(into, got_ref[:, width : main * HEAD_DIM], preferred_element_type=f32)
    first_width = first.shape[1]
    queries_ref[:, :first_width] = first.astype(bf16)
    extras = jnp.zeros((rows, main // 3 * HEAD_DIM), f32)
    for m in range(3):
        extras = extras + jnp.dot(
            late[m], tile_columns(got_ref, range(m, main, 3)), preferred_element_type=f32
        )
    extras = extras.astype(bf16)
    queries_ref[:, first_width:] = extras[:, : width - first_width]
    values_ref[...] = extras[:, width - first_width :]


def attend_kernel(
    start_ref, q_ref, k0_ref, k1_ref, k2_ref, pick_ref, prob_ref,
    g0_ref, g1_ref, g2_ref, loss_ref, weight_ref, spot_scr, prob_scr,
):
    bf16, f32 = jnp.bfloat16, jnp.float32
    rows = q_ref.shape[0]
    kv_count = k0_ref.shape[1] // HEAD_DIM
    heads = q_ref.shape[1] // HEAD_DIM
    group = heads // kv_count
    top = pick_ref.shape[1] // heads
    window = SPAN * rows
    scaling = HEAD_DIM ** (-0.5)
    query = lax.broadcasted_iota(jnp.int32, (1, rows), 1).astype(f32)
    start = start_ref[...].astype(f32)
    reach = query - start + 1.0
    picked = pick_ref[...].astype(f32).T
    rest = picked - jnp.floor(picked / reach) * reach
    rest = jnp.where(rest < 0.0, rest + reach, rest)
    rest = jnp.where(rest >= reach, rest - reach, rest)
    spot = start + rest
    spot_scr[...] = jnp.where(spot < 0.0, spot + window, spot)
    prob_all = prob_ref[...].T
    prob_scr[...] = prob_all
    entropy = jnp.sum(prob_all * jnp.log(prob_all), axis=0, keepdims=True)
    spots = lax.broadcasted_iota(jnp.int32, (window, rows), 0).astype(f32)
    across = lax.broadcasted_iota(jnp.int32, (window, rows), 1).astype(f32)
    position = jnp.where(spots <= across, spots, spots - window)
    allowed = position >= start
    near = spots[:rows] <= across[:rows]

    def parted(rows_of):
        low = rows_of[:rows]
        return jnp.concatenate(
            [jnp.where(near, low, 0.0), jnp.where(near, 0.0, low), rows_of[rows:]], axis=0
        ).astype(bf16)

    def one_group(g, loss):
        lanes = pl.ds(pl.multiple_of(g * HEAD_DIM, HEAD_DIM), HEAD_DIM)
        queries = jnp.concatenate(
            [
                q_ref[:, pl.ds(pl.multiple_of((g * group + i) * HEAD_DIM, HEAD_DIM), HEAD_DIM)]
                for i in range(group)
            ],
            axis=0,
        )
        keys = jnp.concatenate([k0_ref[:, lanes], k2_ref[:, lanes], k1_ref[:, lanes]], axis=0)
        dots = lax.dot_general(
            keys, queries, (((1,), (1,)), ((), ())), preferred_element_type=f32
        )
        slopes = []
        for i in range(group):
            mine = dots[:, i * rows : (i + 1) * rows]
            score = (
                jnp.concatenate(
                    [jnp.where(near, mine[:rows], mine[rows : 2 * rows]), mine[2 * rows :]], axis=0
                )
                * scaling
            )
            held = jnp.where(allowed, score, negative)
            peak = jnp.max(held, axis=0, keepdims=True)
            raised = jnp.exp(held - peak)
            total = jnp.sum(raised, axis=0, keepdims=True)
            weight = raised * (1.0 / total)
            labels = pl.ds(pl.multiple_of((g * group + i) * top, top), top)
            spot_rows, prob_rows = spot_scr[labels, :], prob_scr[labels, :]
            table = jnp.zeros((window, rows), f32)
            for k in range(top):
                table = table + jnp.where(
                    spots == spot_rows[k : k + 1], prob_rows[k : k + 1], 0.0
                )
            mass = jnp.sum(prob_rows, axis=0, keepdims=True)
            loss = loss + mass * (peak + jnp.log(total))
            loss = loss - jnp.sum(table * score, axis=0, keepdims=True)
            weight_ref[g, :, i * rows : (i + 1) * rows] = parted(weight)
            slopes.append(parted((weight * mass - table) * (1.0 / heads)))
        grads = jnp.dot(
            jnp.concatenate(slopes, axis=1), queries, preferred_element_type=f32
        ) * scaling
        g0_ref[:, lanes] = grads[:rows]
        g2_ref[:, lanes] = grads[rows : 2 * rows].astype(bf16)
        g1_ref[:, lanes] = grads[2 * rows :].astype(bf16)
        return loss

    loss = lax.fori_loop(0, kv_count, one_group, entropy)
    loss_ref[...] = loss * (1.0 / heads)


def output_kernel(weight_ref, v0_ref, v1_ref, v2_ref, out_ref):
    bf16, f32 = jnp.bfloat16, jnp.float32
    rows = v0_ref.shape[0]
    group = weight_ref.shape[2] // rows
    for g in range(weight_ref.shape[0]):
        lanes = slice(g * HEAD_DIM, (g + 1) * HEAD_DIM)
        values = jnp.concatenate([v0_ref[:, lanes], v2_ref[:, lanes], v1_ref[:, lanes]], axis=0)
        flipped = jnp.dot(
            values.astype(f32).T.astype(bf16), weight_ref[g], preferred_element_type=f32
        )
        for i in range(group):
            h = g * group + i
            out_ref[:, h * HEAD_DIM : (h + 1) * HEAD_DIM] = (
                flipped[:, i * rows : (i + 1) * rows].T.astype(bf16)
            )


def attend(start, queries, keys, pick, prob):
    rows, kv_width = keys[0].shape
    kv_count = kv_width // HEAD_DIM
    group = queries.shape[1] // kv_width
    bf16, f32 = jnp.bfloat16, jnp.float32
    struct = jax.ShapeDtypeStruct
    return pl.pallas_call(
        attend_kernel,
        out_shape=[
            struct((rows, kv_width), f32),
            struct((rows, kv_width), bf16),
            struct((rows, kv_width), bf16),
            struct((1, rows), f32),
            struct((kv_count, (SPAN + 1) * rows, group * rows), bf16),
        ],
        in_specs=whole(7),
        out_specs=whole(5),
        scratch_shapes=[pltpu.VMEM(pick.shape[::-1], f32)] * 2,
        compiler_params=GRANT,
        name="attend",
    )(start.reshape(1, rows), queries, *keys, pick, prob)


def attend_output(weights, values):
    rows = values[0].shape[0]
    heads = weights.shape[0] * weights.shape[2] // rows
    return pl.pallas_call(
        output_kernel,
        out_shape=jax.ShapeDtypeStruct((rows, heads * HEAD_DIM), jnp.bfloat16),
        in_specs=whole(4),
        out_specs=whole()[0],
        compiler_params=GRANT,
        name="attend_output",
    )(weights, *values)


def whole(count=1):
    return [pl.BlockSpec(memory_space=pltpu.VMEM)] * count


def pack_rows(hidden, queries, values, row_target, seq_count):
    rows = hidden.shape[0]
    tiles = (hidden.shape[1] + queries.shape[1] + values.shape[1]) // HEAD_DIM
    main = tiles - tiles // 4
    return pl.pallas_call(
        pack_kernel,
        out_shape=jax.ShapeDtypeStruct((seq_count * 8, (main + 1) * HEAD_DIM), jnp.bfloat16),
        in_specs=whole(4),
        out_specs=whole()[0],
        compiler_params=GRANT,
        name="pack_rows",
    )(row_target.reshape(1, rows), hidden, queries, values)


def project(got, place_of, own_half, other_half, cosine, sine, sides):
    rows, (width, kv_width) = cosine.shape[0], own_half.shape
    struct = jax.ShapeDtypeStruct
    return pl.pallas_call(
        functools.partial(project_kernel, sides),
        out_shape=[struct((rows, w), jnp.bfloat16) for w in (kv_width, width, width)],
        in_specs=[pl.BlockSpec(memory_space=pltpu.SMEM)] + whole(5),
        out_specs=whole(3),
        scratch_shapes=[pltpu.VMEM((rows, width), jnp.bfloat16)] * 2,
        compiler_params=GRANT,
        name="project",
    )(place_of, got, own_half, other_half, cosine, sine)


def unpack_rest(got, rows, width, kv_width):
    return pl.pallas_call(
        rest_kernel,
        out_shape=[jax.ShapeDtypeStruct((rows, w), jnp.bfloat16) for w in (width, kv_width)],
        in_specs=whole(),
        out_specs=whole(2),
        compiler_params=GRANT,
        name="unpack_rest",
    )(got)


def step(
    hidden, queries, values, row_target, key_weight, dialogue_lengths, teacher_pick, teacher_prob
):
    bf16, f32 = jnp.bfloat16, jnp.float32
    local_rows, width = hidden.shape
    seq_count = lax.axis_size(SEQ)
    seq_index = lax.axis_index(SEQ)
    lines = lax.axis_size("y")
    device_count = seq_count * lines * lax.axis_size("core")
    kv_width = values.shape[1]

    place_of = jnp.stack([lax.axis_index("core"), lax.axis_index("y")]).astype(jnp.int32)

    plane_rows = exchange(jnp.broadcast_to(key_weight, (seq_count,) + key_weight.shape), SEQ)
    plane_rows = plane_rows.reshape(local_rows, kv_width)
    turned = [plane_rows]
    for by in range(1, lines):
        turned.append(line_shift(plane_rows, by))
    own_half = jnp.concatenate(turned, axis=0)
    other_half = core_swap(own_half)

    parcels = pack_rows(hidden, queries, values, row_target, seq_count)
    received = exchange(parcels.reshape(seq_count, 8, -1), SEQ)
    got = received.reshape(seq_count * 8, -1)
    positions = seq_index * local_rows + jnp.arange(local_rows, dtype=jnp.int32)
    cosine, sine = turn_angles(positions)
    keys_seq, mine, theirs = project(
        got,
        place_of,
        own_half,
        other_half,
        jnp.concatenate([cosine[:, 0], cosine[:, 0]], axis=1),
        jnp.concatenate([-sine[:, 0], sine[:, 0]], axis=1),
        lax.axis_size(ACROSS),
    )
    queries_seq, values_seq = unpack_rest(got, local_rows, width, kv_width)

    starts = dialogue_starts(dialogue_lengths[0], positions)
    near_keys = [seq_shift(keys_seq, by) for by in range(1, SPAN + 1)]
    values_late, *near_keys = lax.optimization_barrier((values_seq, *near_keys))
    values_all = [values_seq]
    for by in range(1, SPAN + 1):
        values_all.append(seq_shift(values_late, by))
    own_grad, grad_1, grad_2, token_loss, weights = attend(
        starts - seq_index * local_rows,
        queries_seq,
        [keys_seq] + near_keys,
        teacher_pick,
        teacher_prob,
    )
    theirs, own_grad = lax.optimization_barrier((theirs, own_grad))
    partner = core_swap(theirs)
    rotated_grad = (
        own_grad + seq_shift(grad_1, -1).astype(f32) + seq_shift(grad_2, -2).astype(f32)
    )
    key_grad = rotate(rotated_grad, cosine, -sine).astype(bf16)

    inverse_root = (local_rows * device_count) ** (-0.5)

    def term(columns, grads):
        return jnp.einsum("td,tc->dc", columns, grads, preferred_element_type=f32)

    summed = (term(mine, key_grad) + term(partner, core_swap(key_grad))).astype(bf16)
    sides = lax.axis_size(ACROSS)
    pieces = jnp.transpose(summed.reshape(lines, sides, -1, kv_width), (1, 0, 2, 3))
    pieces = pieces.reshape(sides, -1, kv_width)
    line = jnp.sum(exchange(pieces, ACROSS).astype(f32), axis=0).astype(bf16)
    attn_out = attend_output(weights, values_all)
    last = exchange(line.reshape(-1, 4, kv_width), ("y", "z"))
    weight_grad = jnp.sum(last.astype(f32), axis=0) * inverse_root
    return (attn_out, token_loss.reshape(local_rows), weight_grad)


def solution(mesh):
    fine = Mesh(np.asarray(mesh.devices).reshape(8, 2, 8, 2, 2), EVERY)
    pack = ("y", "core")
    placed = (
        P(EVERY, None),
        P(EVERY, None),
        P(EVERY, None),
        P(EVERY),
        P(EVERY, None),
        P(pack, None),
        P(EVERY, None),
        P(EVERY, None),
    )
    return jax.shard_map(
        step,
        mesh=fine,
        in_specs=placed,
        out_specs=(P(EVERY, None), P(EVERY), P(EVERY, None)),
        check_vma=False,
    )
```

```python
import jax
import jax.numpy as jnp
import numpy as np
from jax import lax
from jax.experimental import pallas as pl
from jax.experimental.pallas import tpu as pltpu
from jax.sharding import Mesh
from jax.sharding import PartitionSpec as P


HEAD_DIM = 128
SPAN = 2
SLOTS = 6

negative = -1e30
rope_base = 500000.0

GRANT = pltpu.CompilerParams(vmem_limit_bytes=24 << 20)

ACROSS = ("xh", "xl")
SEQ = ("z",) + ACROSS
EVERY = ("y", "core") + SEQ


def exchange(pieces, axes):
    return lax.all_to_all(pieces, axes, split_axis=0, concat_axis=0, tiled=True)


def seq_shift(shard, by):
    devices = lax.axis_size(SEQ)
    pairs = [(i, i + by) for i in range(devices) if 0 <= i + by < devices]
    return lax.ppermute(shard, SEQ, pairs)


def line_shift(shard, by):
    devices = lax.axis_size("y")
    return lax.ppermute(shard, "y", [(i, (i + by) % devices) for i in range(devices)])


def core_swap(shard):
    return lax.ppermute(shard, "core", [(0, 1), (1, 0)])


def turn_angles(positions):
    halfway = HEAD_DIM // 2
    frequency = rope_base ** (-2.0 * jnp.arange(halfway, dtype=jnp.float32) / HEAD_DIM)
    angle = positions.astype(jnp.float32)[:, None] * frequency[None, :]
    return jnp.cos(angle)[:, None, :], jnp.sin(angle)[:, None, :]


def rotate(matrix, cosine, sine):
    count = matrix.shape[0]
    halfway = HEAD_DIM // 2
    split = matrix.reshape(count, -1, HEAD_DIM)
    first_half = split[..., :halfway]
    second_half = split[..., halfway:]
    joined = jnp.concatenate(
        [first_half * cosine - second_half * sine, second_half * cosine + first_half * sine],
        axis=-1,
    )
    return joined.reshape(count, -1)


def dialogue_starts(lengths, positions):
    ending = jnp.cumsum(lengths)
    picked = jnp.where(ending[None, :] <= positions[:, None], lengths[None, :], 0)
    return jnp.sum(picked, axis=1)


def pack_kernel(target_ref, hidden_ref, queries_ref, values_ref, out_ref):
    bf16, f32 = jnp.bfloat16, jnp.float32
    rows = hidden_ref.shape[0]
    parcels = out_ref.shape[0]
    main = out_ref.shape[1] // HEAD_DIM - 1
    third = main // 3
    refs = (hidden_ref, queries_ref, values_ref)
    tiles = [ref[:, i * HEAD_DIM : (i + 1) * HEAD_DIM] for ref in refs for i in range(ref.shape[1] // HEAD_DIM)]
    target = target_ref[...]
    block = target // rows
    offset = (target - block * rows - rows).astype(f32)
    across = jnp.broadcast_to(block.astype(f32), (rows, rows))
    down = across.T
    first = lax.broadcasted_iota(jnp.int32, (rows, rows), 0)
    second = lax.broadcasted_iota(jnp.int32, (rows, rows), 1)
    rank = jnp.sum(jnp.where((across == down) & (first < second), 1.0, 0.0), axis=0, keepdims=True)
    rank = rank.astype(jnp.int32)
    row = lax.broadcasted_iota(jnp.int32, (parcels, rows), 0)
    place = row % 8
    to_block = block == row // 8
    low = jnp.where(to_block & (place == rank) & (place < SLOTS), 1.0, 0.0)
    lane = lax.broadcasted_iota(jnp.int32, (parcels, HEAD_DIM), 1)
    meta = jnp.zeros((parcels, HEAD_DIM), f32)
    extras = jnp.concatenate(tiles[main:], axis=1)
    for m in range(3):
        high = jnp.where(
            to_block & (place - SLOTS + 2 * m == rank) & (place >= SLOTS), 1.0, 0.0
        )
        place_of = jnp.sum((low + high) * offset, axis=1, keepdims=True) + rows
        meta = jnp.where(lane == m, place_of, meta)
        select = jnp.concatenate([low, high], axis=1).astype(bf16)
        both = jnp.concatenate([jnp.concatenate(tiles[m:main:3], axis=1), extras], axis=0)
        done = jnp.dot(select, both, preferred_element_type=f32).astype(bf16)
        for i in range(third):
            g = 3 * i + m
            out_ref[:, g * HEAD_DIM : (g + 1) * HEAD_DIM] = done[:, i * HEAD_DIM : (i + 1) * HEAD_DIM]
    out_ref[:, main * HEAD_DIM :] = meta.astype(bf16)


def tile_columns(ref, indices):
    return jnp.concatenate([ref[:, g * HEAD_DIM : (g + 1) * HEAD_DIM] for g in indices], axis=1)


def arrivals(got_ref, rows):
    parcels = got_ref.shape[0]
    main = got_ref.shape[1] // HEAD_DIM - 1
    meta = got_ref[:, main * HEAD_DIM :].astype(jnp.float32).T
    token = lax.broadcasted_iota(jnp.int32, (rows, parcels), 0).astype(jnp.float32)
    low = lax.broadcasted_iota(jnp.int32, (rows, parcels), 1) % 8 < SLOTS
    hits = [meta[m : m + 1, :] == token for m in range(3)]
    into = jnp.where(hits[0] & low, 1.0, 0.0).astype(jnp.bfloat16)
    late = [jnp.where(hit & ~low, 1.0, 0.0).astype(jnp.bfloat16) for hit in hits]
    return main, into, late


def project_kernel(
    place_ref, got_ref, own_ref, other_ref, cosine_ref, sine_ref,
    keys_ref, mine_ref, theirs_ref, mine_turned, theirs_turned,
):
    bf16, f32 = jnp.bfloat16, jnp.float32
    rows = mine_ref.shape[0]
    count = mine_ref.shape[1] // HEAD_DIM
    _, into, _ = arrivals(got_ref, rows)
    done = jnp.dot(into, got_ref[:, : 2 * count * HEAD_DIM], preferred_element_type=f32)
    is_first = jnp.broadcast_to(place_ref[0], (rows, HEAD_DIM)) == 0
    for i in range(count):
        even = done[:, 2 * i * HEAD_DIM : (2 * i + 1) * HEAD_DIM]
        odd = done[:, (2 * i + 1) * HEAD_DIM : (2 * i + 2) * HEAD_DIM]
        own = jnp.where(is_first, even, odd).astype(bf16)
        other = jnp.where(is_first, odd, even).astype(bf16)
        mine_ref[:, i * HEAD_DIM : (i + 1) * HEAD_DIM] = own
        theirs_ref[:, i * HEAD_DIM : (i + 1) * HEAD_DIM] = other
        turned = lax.rem(place_ref[1] - i + count, count)
        lanes = pl.ds(pl.multiple_of(turned * HEAD_DIM, HEAD_DIM), HEAD_DIM)
        mine_turned[:, lanes] = own
        theirs_turned[:, lanes] = other
    keys = jnp.dot(mine_turned[...], own_ref[...], preferred_element_type=f32)
    keys = keys + jnp.dot(theirs_turned[...], other_ref[...], preferred_element_type=f32)
    for h in range(keys.shape[1] // HEAD_DIM):
        head = keys[:, h * HEAD_DIM : (h + 1) * HEAD_DIM]
        swapped = pltpu.roll(head, HEAD_DIM // 2, 1)
        keys_ref[:, h * HEAD_DIM : (h + 1) * HEAD_DIM] = (
            head * cosine_ref[...] + swapped * sine_ref[...]
        ).astype(bf16)


def rest_kernel(got_ref, queries_ref, values_ref):
    bf16, f32 = jnp.bfloat16, jnp.float32
    rows, width = queries_ref.shape
    main, into, late = arrivals(got_ref, rows)
    first = jnp.dot(into, got_ref[:, width : main * HEAD_DIM], preferred_element_type=f32)
    first_width = first.shape[1]
    queries_ref[:, :first_width] = first.astype(bf16)
    extras = jnp.zeros((rows, main // 3 * HEAD_DIM), f32)
    for m in range(3):
        extras = extras + jnp.dot(
            late[m], tile_columns(got_ref, range(m, main, 3)), preferred_element_type=f32
        )
    extras = extras.astype(bf16)
    queries_ref[:, first_width:] = extras[:, : width - first_width]
    values_ref[...] = extras[:, width - first_width :]


def attend_kernel(
    start_ref, q_ref, k0_ref, k1_ref, k2_ref, pick_ref, prob_ref,
    g0_ref, g1_ref, g2_ref, loss_ref, weight_ref, spot_scr, prob_scr,
):
    bf16, f32 = jnp.bfloat16, jnp.float32
    rows = q_ref.shape[0]
    kv_count = k0_ref.shape[1] // HEAD_DIM
    heads = q_ref.shape[1] // HEAD_DIM
    group = heads // kv_count
    top = pick_ref.shape[1] // heads
    window = SPAN * rows
    scaling = HEAD_DIM ** (-0.5)
    query = lax.broadcasted_iota(jnp.int32, (1, rows), 1).astype(f32)
    start = start_ref[...].astype(f32)
    reach = query - start + 1.0
    picked = pick_ref[...].astype(f32).T
    rest = picked - jnp.floor(picked / reach) * reach
    rest = jnp.where(rest < 0.0, rest + reach, rest)
    rest = jnp.where(rest >= reach, rest - reach, rest)
    spot = start + rest
    spot_scr[...] = jnp.where(spot < 0.0, spot + window, spot)
    prob_all = prob_ref[...].T
    prob_scr[...] = prob_all
    entropy = jnp.sum(prob_all * jnp.log(prob_all), axis=0, keepdims=True)
    spots = lax.broadcasted_iota(jnp.int32, (window, rows), 0).astype(f32)
    across = lax.broadcasted_iota(jnp.int32, (window, rows), 1).astype(f32)
    position = jnp.where(spots <= across, spots, spots - window)
    allowed = position >= start
    near = spots[:rows] <= across[:rows]

    def parted(rows_of):
        low = rows_of[:rows]
        return jnp.concatenate(
            [jnp.where(near, low, 0.0), jnp.where(near, 0.0, low), rows_of[rows:]], axis=0
        ).astype(bf16)

    def one_group(g, loss):
        lanes = pl.ds(pl.multiple_of(g * HEAD_DIM, HEAD_DIM), HEAD_DIM)
        queries = jnp.concatenate(
            [
                q_ref[:, pl.ds(pl.multiple_of((g * group + i) * HEAD_DIM, HEAD_DIM), HEAD_DIM)]
                for i in range(group)
            ],
            axis=0,
        )
        keys = jnp.concatenate([k0_ref[:, lanes], k2_ref[:, lanes], k1_ref[:, lanes]], axis=0)
        dots = lax.dot_general(
            keys, queries, (((1,), (1,)), ((), ())), preferred_element_type=f32
        )
        slopes = []
        for i in range(group):
            mine = dots[:, i * rows : (i + 1) * rows]
            score = (
                jnp.concatenate(
                    [jnp.where(near, mine[:rows], mine[rows : 2 * rows]), mine[2 * rows :]], axis=0
                )
                * scaling
            )
            held = jnp.where(allowed, score, negative)
            peak = jnp.max(held, axis=0, keepdims=True)
            raised = jnp.exp(held - peak)
            total = jnp.sum(raised, axis=0, keepdims=True)
            weight = raised * (1.0 / total)
            labels = pl.ds(pl.multiple_of((g * group + i) * top, top), top)
            spot_rows, prob_rows = spot_scr[labels, :], prob_scr[labels, :]
            table = jnp.zeros((window, rows), f32)
            for k in range(top):
                table = table + jnp.where(
                    spots == spot_rows[k : k + 1], prob_rows[k : k + 1], 0.0
                )
            mass = jnp.sum(prob_rows, axis=0, keepdims=True)
            loss = loss + mass * (peak + jnp.log(total))
            loss = loss - jnp.sum(table * score, axis=0, keepdims=True)
            weight_ref[g, :, i * rows : (i + 1) * rows] = parted(weight)
            slopes.append(parted((weight * mass - table) * (1.0 / heads)))
        grads = jnp.dot(
            jnp.concatenate(slopes, axis=1), queries, preferred_element_type=f32
        ) * scaling
        g0_ref[:, lanes] = grads[:rows]
        g2_ref[:, lanes] = grads[rows : 2 * rows].astype(bf16)
        g1_ref[:, lanes] = grads[2 * rows :].astype(bf16)
        return loss

    loss = lax.fori_loop(0, kv_count, one_group, entropy)
    loss_ref[...] = loss * (1.0 / heads)


def output_kernel(weight_ref, v0_ref, v1_ref, v2_ref, out_ref):
    bf16, f32 = jnp.bfloat16, jnp.float32
    rows = v0_ref.shape[0]
    group = weight_ref.shape[2] // rows
    for g in range(weight_ref.shape[0]):
        lanes = slice(g * HEAD_DIM, (g + 1) * HEAD_DIM)
        values = jnp.concatenate([v0_ref[:, lanes], v2_ref[:, lanes], v1_ref[:, lanes]], axis=0)
        flipped = jnp.dot(
            values.astype(f32).T.astype(bf16), weight_ref[g], preferred_element_type=f32
        )
        for i in range(group):
            h = g * group + i
            out_ref[:, h * HEAD_DIM : (h + 1) * HEAD_DIM] = (
                flipped[:, i * rows : (i + 1) * rows].T.astype(bf16)
            )


def attend(start, queries, keys, pick, prob):
    rows, kv_width = keys[0].shape
    kv_count = kv_width // HEAD_DIM
    group = queries.shape[1] // kv_width
    bf16, f32 = jnp.bfloat16, jnp.float32
    struct = jax.ShapeDtypeStruct
    return pl.pallas_call(
        attend_kernel,
        out_shape=[
            struct((rows, kv_width), f32),
            struct((rows, kv_width), bf16),
            struct((rows, kv_width), bf16),
            struct((1, rows), f32),
            struct((kv_count, (SPAN + 1) * rows, group * rows), bf16),
        ],
        in_specs=whole(7),
        out_specs=whole(5),
        scratch_shapes=[pltpu.VMEM(pick.shape[::-1], f32)] * 2,
        compiler_params=GRANT,
        name="attend",
    )(start.reshape(1, rows), queries, *keys, pick, prob)


def attend_output(weights, values):
    rows = values[0].shape[0]
    heads = weights.shape[0] * weights.shape[2] // rows
    return pl.pallas_call(
        output_kernel,
        out_shape=jax.ShapeDtypeStruct((rows, heads * HEAD_DIM), jnp.bfloat16),
        in_specs=whole(4),
        out_specs=whole()[0],
        compiler_params=GRANT,
        name="attend_output",
    )(weights, *values)


def whole(count=1):
    return [pl.BlockSpec(memory_space=pltpu.VMEM)] * count


def pack_rows(hidden, queries, values, row_target, seq_count):
    rows = hidden.shape[0]
    tiles = (hidden.shape[1] + queries.shape[1] + values.shape[1]) // HEAD_DIM
    main = tiles - tiles // 4
    return pl.pallas_call(
        pack_kernel,
        out_shape=jax.ShapeDtypeStruct((seq_count * 8, (main + 1) * HEAD_DIM), jnp.bfloat16),
        in_specs=whole(4),
        out_specs=whole()[0],
        compiler_params=GRANT,
        name="pack_rows",
    )(row_target.reshape(1, rows), hidden, queries, values)


def project(got, place_of, own_half, other_half, cosine, sine):
    rows, (width, kv_width) = cosine.shape[0], own_half.shape
    struct = jax.ShapeDtypeStruct
    return pl.pallas_call(
        project_kernel,
        out_shape=[struct((rows, w), jnp.bfloat16) for w in (kv_width, width, width)],
        in_specs=[pl.BlockSpec(memory_space=pltpu.SMEM)] + whole(5),
        out_specs=whole(3),
        scratch_shapes=[pltpu.VMEM((rows, width), jnp.bfloat16)] * 2,
        compiler_params=GRANT,
        name="project",
    )(place_of, got, own_half, other_half, cosine, sine)


def unpack_rest(got, rows, width, kv_width):
    return pl.pallas_call(
        rest_kernel,
        out_shape=[jax.ShapeDtypeStruct((rows, w), jnp.bfloat16) for w in (width, kv_width)],
        in_specs=whole(),
        out_specs=whole(2),
        compiler_params=GRANT,
        name="unpack_rest",
    )(got)


def step(
    hidden, queries, values, row_target, key_weight, dialogue_lengths, teacher_pick, teacher_prob
):
    bf16, f32 = jnp.bfloat16, jnp.float32
    local_rows, width = hidden.shape
    seq_count = lax.axis_size(SEQ)
    seq_index = lax.axis_index(SEQ)
    lines = lax.axis_size("y")
    device_count = seq_count * lines * lax.axis_size("core")
    kv_width = values.shape[1]

    place_of = jnp.stack([lax.axis_index("core"), lax.axis_index("y")]).astype(jnp.int32)

    plane_rows = exchange(jnp.broadcast_to(key_weight, (seq_count,) + key_weight.shape), SEQ)
    plane_rows = plane_rows.reshape(local_rows, kv_width)
    turned = [plane_rows]
    for by in range(1, lines):
        turned.append(line_shift(plane_rows, by))
    own_half = jnp.concatenate(turned, axis=0)
    other_half = core_swap(own_half)

    parcels = pack_rows(hidden, queries, values, row_target, seq_count)
    received = exchange(parcels.reshape(seq_count, 8, -1), SEQ)
    got = received.reshape(seq_count * 8, -1)
    positions = seq_index * local_rows + jnp.arange(local_rows, dtype=jnp.int32)
    cosine, sine = turn_angles(positions)
    keys_seq, mine, theirs = project(
        got,
        place_of,
        own_half,
        other_half,
        jnp.concatenate([cosine[:, 0], cosine[:, 0]], axis=1),
        jnp.concatenate([-sine[:, 0], sine[:, 0]], axis=1),
    )
    queries_seq, values_seq = unpack_rest(got, local_rows, width, kv_width)

    starts = dialogue_starts(dialogue_lengths[0], positions)
    near_keys = []
    for by in range(1, SPAN + 1):
        near_keys.append(seq_shift(keys_seq, by))
    own_grad, grad_1, grad_2, token_loss, weights = attend(
        starts - seq_index * local_rows,
        queries_seq,
        [keys_seq] + near_keys,
        teacher_pick,
        teacher_prob,
    )
    theirs, own_grad = lax.optimization_barrier((theirs, own_grad))
    partner = core_swap(theirs)
    rotated_grad = (
        own_grad + seq_shift(grad_1, -1).astype(f32) + seq_shift(grad_2, -2).astype(f32)
    )
    key_grad = rotate(rotated_grad, cosine, -sine).astype(bf16)

    inverse_root = (local_rows * device_count) ** (-0.5)

    def term(columns, grads):
        return jnp.einsum("td,tc->dc", columns, grads, preferred_element_type=f32)

    summed = (term(mine, key_grad) + term(partner, core_swap(key_grad))).astype(bf16)
    values_late, pieces = lax.optimization_barrier(
        (values_seq, summed.reshape(lines * lax.axis_size("z"), -1, kv_width))
    )
    line = jnp.sum(exchange(pieces, ("y", "z")).astype(f32), axis=0)
    values_all = [values_seq] + [seq_shift(values_late, by) for by in range(1, SPAN + 1)]
    attn_out = attend_output(weights, values_all)
    last = exchange(line.reshape(lax.axis_size(ACROSS), -1, kv_width), ACROSS)
    weight_grad = jnp.sum(last, axis=0) * inverse_root
    return (attn_out, token_loss.reshape(local_rows), weight_grad)


def solution(mesh):
    fine = Mesh(np.asarray(mesh.devices).reshape(8, 2, 8, 2, 2), EVERY)
    pack = ("y", "core")
    placed = (
        P(EVERY, None),
        P(EVERY, None),
        P(EVERY, None),
        P(EVERY),
        P(EVERY, None),
        P(pack, None),
        P(EVERY, None),
        P(EVERY, None),
    )
    return jax.shard_map(
        step,
        mesh=fine,
        in_specs=placed,
        out_specs=(P(EVERY, None), P(EVERY), P(EVERY, None)),
        check_vma=False,
    )
```

```python
import functools

import jax
import jax.numpy as jnp
import numpy as np
from jax import lax
from jax.experimental import pallas as pl
from jax.experimental.pallas import tpu as pltpu
from jax.sharding import Mesh
from jax.sharding import PartitionSpec as P


HEAD_DIM = 128
SPAN = 2
SLOTS = 6

negative = -1e30
rope_base = 500000.0

GRANT = pltpu.CompilerParams(vmem_limit_bytes=24 << 20)

ACROSS = ("xh", "xl")
SEQ = ("z",) + ACROSS
EVERY = ("y", "core") + SEQ


def exchange(pieces, axes):
    return lax.all_to_all(pieces, axes, split_axis=0, concat_axis=0, tiled=True)


def seq_shift(shard, by):
    devices = lax.axis_size(SEQ)
    pairs = [(i, i + by) for i in range(devices) if 0 <= i + by < devices]
    return lax.ppermute(shard, SEQ, pairs)


def line_shift(shard, by):
    devices = lax.axis_size("y")
    return lax.ppermute(shard, "y", [(i, (i + by) % devices) for i in range(devices)])


def core_swap(shard):
    return lax.ppermute(shard, "core", [(0, 1), (1, 0)])


def turn_angles(positions):
    halfway = HEAD_DIM // 2
    frequency = rope_base ** (-2.0 * jnp.arange(halfway, dtype=jnp.float32) / HEAD_DIM)
    angle = positions.astype(jnp.float32)[:, None] * frequency[None, :]
    return jnp.cos(angle)[:, None, :], jnp.sin(angle)[:, None, :]


def rotate(matrix, cosine, sine):
    count = matrix.shape[0]
    halfway = HEAD_DIM // 2
    split = matrix.reshape(count, -1, HEAD_DIM)
    first_half = split[..., :halfway]
    second_half = split[..., halfway:]
    joined = jnp.concatenate(
        [first_half * cosine - second_half * sine, second_half * cosine + first_half * sine],
        axis=-1,
    )
    return joined.reshape(count, -1)


def dialogue_starts(lengths, positions):
    ending = jnp.cumsum(lengths)
    picked = jnp.where(ending[None, :] <= positions[:, None], lengths[None, :], 0)
    return jnp.sum(picked, axis=1)


def pack_kernel(target_ref, hidden_ref, queries_ref, values_ref, out_ref):
    bf16, f32 = jnp.bfloat16, jnp.float32
    rows = hidden_ref.shape[0]
    parcels = out_ref.shape[0]
    main = out_ref.shape[1] // HEAD_DIM - 1
    third = main // 3
    refs = (hidden_ref, queries_ref, values_ref)
    tiles = [ref[:, i * HEAD_DIM : (i + 1) * HEAD_DIM] for ref in refs for i in range(ref.shape[1] // HEAD_DIM)]
    target = target_ref[...]
    block = target // rows
    offset = (target - block * rows - rows).astype(f32)
    across = jnp.broadcast_to(block.astype(f32), (rows, rows))
    down = across.T
    first = lax.broadcasted_iota(jnp.int32, (rows, rows), 0)
    second = lax.broadcasted_iota(jnp.int32, (rows, rows), 1)
    rank = jnp.sum(jnp.where((across == down) & (first < second), 1.0, 0.0), axis=0, keepdims=True)
    rank = rank.astype(jnp.int32)
    row = lax.broadcasted_iota(jnp.int32, (parcels, rows), 0)
    place = row % 8
    to_block = block == row // 8
    low = jnp.where(to_block & (place == rank) & (place < SLOTS), 1.0, 0.0)
    lane = lax.broadcasted_iota(jnp.int32, (parcels, HEAD_DIM), 1)
    meta = jnp.zeros((parcels, HEAD_DIM), f32)
    extras = jnp.concatenate(tiles[main:], axis=1)
    for m in range(3):
        high = jnp.where(
            to_block & (place - SLOTS + 2 * m == rank) & (place >= SLOTS), 1.0, 0.0
        )
        place_of = jnp.sum((low + high) * offset, axis=1, keepdims=True) + rows
        meta = jnp.where(lane == m, place_of, meta)
        select = jnp.concatenate([low, high], axis=1).astype(bf16)
        both = jnp.concatenate([jnp.concatenate(tiles[m:main:3], axis=1), extras], axis=0)
        done = jnp.dot(select, both, preferred_element_type=f32).astype(bf16)
        for i in range(third):
            g = 3 * i + m
            out_ref[:, g * HEAD_DIM : (g + 1) * HEAD_DIM] = done[:, i * HEAD_DIM : (i + 1) * HEAD_DIM]
    out_ref[:, main * HEAD_DIM :] = meta.astype(bf16)


def tile_columns(ref, indices):
    return jnp.concatenate([ref[:, g * HEAD_DIM : (g + 1) * HEAD_DIM] for g in indices], axis=1)


def arrivals(got_ref, rows):
    parcels = got_ref.shape[0]
    main = got_ref.shape[1] // HEAD_DIM - 1
    meta = got_ref[:, main * HEAD_DIM :].astype(jnp.float32).T
    token = lax.broadcasted_iota(jnp.int32, (rows, parcels), 0).astype(jnp.float32)
    low = lax.broadcasted_iota(jnp.int32, (rows, parcels), 1) % 8 < SLOTS
    hits = [meta[m : m + 1, :] == token for m in range(3)]
    into = jnp.where(hits[0] & low, 1.0, 0.0).astype(jnp.bfloat16)
    late = [jnp.where(hit & ~low, 1.0, 0.0).astype(jnp.bfloat16) for hit in hits]
    return main, into, late


def project_kernel(
    sides, place_ref, got_ref, own_ref, other_ref, cosine_ref, sine_ref,
    keys_ref, mine_ref, theirs_ref, mine_turned, theirs_turned,
):
    bf16, f32 = jnp.bfloat16, jnp.float32
    rows = mine_ref.shape[0]
    count = mine_ref.shape[1] // HEAD_DIM
    _, into, _ = arrivals(got_ref, rows)
    done = jnp.dot(into, got_ref[:, : 2 * count * HEAD_DIM], preferred_element_type=f32)
    is_first = jnp.broadcast_to(place_ref[0], (rows, HEAD_DIM)) == 0
    own_tiles, other_tiles = [], []
    for i in range(count):
        even = done[:, 2 * i * HEAD_DIM : (2 * i + 1) * HEAD_DIM]
        odd = done[:, (2 * i + 1) * HEAD_DIM : (2 * i + 2) * HEAD_DIM]
        own = jnp.where(is_first, even, odd).astype(bf16)
        other = jnp.where(is_first, odd, even).astype(bf16)
        own_tiles.append(own)
        other_tiles.append(other)
        turned = lax.rem(place_ref[1] - i + count, count)
        lanes = pl.ds(pl.multiple_of(turned * HEAD_DIM, HEAD_DIM), HEAD_DIM)
        mine_turned[:, lanes] = own
        theirs_turned[:, lanes] = other
    keys = jnp.dot(mine_turned[...], own_ref[...], preferred_element_type=f32)
    keys = keys + jnp.dot(theirs_turned[...], other_ref[...], preferred_element_type=f32)
    for h in range(keys.shape[1] // HEAD_DIM):
        head = keys[:, h * HEAD_DIM : (h + 1) * HEAD_DIM]
        swapped = pltpu.roll(head, HEAD_DIM // 2, 1)
        keys_ref[:, h * HEAD_DIM : (h + 1) * HEAD_DIM] = (
            head * cosine_ref[...] + swapped * sine_ref[...]
        ).astype(bf16)
    source = lax.broadcasted_iota(jnp.int32, (HEAD_DIM, HEAD_DIM), 0)
    target = lax.broadcasted_iota(jnp.int32, (HEAD_DIM, HEAD_DIM), 1)
    part = HEAD_DIM // sides
    wanted = (target % part) // 4 * (4 * sides) + target // part * 4 + target % 4
    order = jnp.where(source == wanted, 1.0, 0.0).astype(bf16)
    for tiles, ref in ((own_tiles, mine_ref), (other_tiles, theirs_ref)):
        moved = jnp.dot(
            jnp.concatenate(tiles, axis=0), order, preferred_element_type=f32
        ).astype(bf16)
        for i in range(count):
            ref[:, i * HEAD_DIM : (i + 1) * HEAD_DIM] = moved[i * rows : (i + 1) * rows]


def rest_kernel(got_ref, queries_ref, values_ref):
    bf16, f32 = jnp.bfloat16, jnp.float32
    rows, width = queries_ref.shape
    main, into, late = arrivals(got_ref, rows)
    first = jnp.dot(into, got_ref[:, width : main * HEAD_DIM], preferred_element_type=f32)
    first_width = first.shape[1]
    queries_ref[:, :first_width] = first.astype(bf16)
    extras = jnp.zeros((rows, main // 3 * HEAD_DIM), f32)
    for m in range(3):
        extras = extras + jnp.dot(
            late[m], tile_columns(got_ref, range(m, main, 3)), preferred_element_type=f32
        )
    extras = extras.astype(bf16)
    queries_ref[:, first_width:] = extras[:, : width - first_width]
    values_ref[...] = extras[:, width - first_width :]


def attend_kernel(
    start_ref, q_ref, k0_ref, k1_ref, k2_ref, pick_ref, prob_ref,
    g0_ref, g1_ref, g2_ref, loss_ref, weight_ref, spot_scr, prob_scr,
):
    bf16, f32 = jnp.bfloat16, jnp.float32
    rows = q_ref.shape[0]
    kv_count = k0_ref.shape[1] // HEAD_DIM
    heads = q_ref.shape[1] // HEAD_DIM
    group = heads // kv_count
    top = pick_ref.shape[1] // heads
    window = SPAN * rows
    scaling = HEAD_DIM ** (-0.5)
    query = lax.broadcasted_iota(jnp.int32, (1, rows), 1).astype(f32)
    start = start_ref[...].astype(f32)
    reach = query - start + 1.0
    picked = pick_ref[...].astype(f32).T
    rest = picked - jnp.floor(picked / reach) * reach
    rest = jnp.where(rest < 0.0, rest + reach, rest)
    rest = jnp.where(rest >= reach, rest - reach, rest)
    spot = start + rest
    spot_scr[...] = jnp.where(spot < 0.0, spot + window, spot)
    prob_all = prob_ref[...].T
    prob_scr[...] = prob_all
    entropy = jnp.sum(prob_all * jnp.log(prob_all), axis=0, keepdims=True)
    spots = lax.broadcasted_iota(jnp.int32, (window, rows), 0).astype(f32)
    across = lax.broadcasted_iota(jnp.int32, (window, rows), 1).astype(f32)
    position = jnp.where(spots <= across, spots, spots - window)
    allowed = position >= start
    near = spots[:rows] <= across[:rows]

    def parted(rows_of):
        low = rows_of[:rows]
        return jnp.concatenate(
            [jnp.where(near, low, 0.0), jnp.where(near, 0.0, low), rows_of[rows:]], axis=0
        ).astype(bf16)

    def one_group(g, loss):
        lanes = pl.ds(pl.multiple_of(g * HEAD_DIM, HEAD_DIM), HEAD_DIM)
        queries = jnp.concatenate(
            [
                q_ref[:, pl.ds(pl.multiple_of((g * group + i) * HEAD_DIM, HEAD_DIM), HEAD_DIM)]
                for i in range(group)
            ],
            axis=0,
        )
        keys = jnp.concatenate([k0_ref[:, lanes], k2_ref[:, lanes], k1_ref[:, lanes]], axis=0)
        dots = lax.dot_general(
            keys, queries, (((1,), (1,)), ((), ())), preferred_element_type=f32
        )
        slopes = []
        for i in range(group):
            mine = dots[:, i * rows : (i + 1) * rows]
            score = (
                jnp.concatenate(
                    [jnp.where(near, mine[:rows], mine[rows : 2 * rows]), mine[2 * rows :]], axis=0
                )
                * scaling
            )
            held = jnp.where(allowed, score, negative)
            peak = jnp.max(held, axis=0, keepdims=True)
            raised = jnp.exp(held - peak)
            total = jnp.sum(raised, axis=0, keepdims=True)
            weight = raised * (1.0 / total)
            labels = pl.ds(pl.multiple_of((g * group + i) * top, top), top)
            spot_rows, prob_rows = spot_scr[labels, :], prob_scr[labels, :]
            table = jnp.zeros((window, rows), f32)
            for k in range(top):
                table = table + jnp.where(
                    spots == spot_rows[k : k + 1], prob_rows[k : k + 1], 0.0
                )
            mass = jnp.sum(prob_rows, axis=0, keepdims=True)
            loss = loss + mass * (peak + jnp.log(total))
            loss = loss - jnp.sum(table * score, axis=0, keepdims=True)
            weight_ref[g, :, i * rows : (i + 1) * rows] = parted(weight)
            slopes.append(parted((weight * mass - table) * (1.0 / heads)))
        grads = jnp.dot(
            jnp.concatenate(slopes, axis=1), queries, preferred_element_type=f32
        ) * scaling
        g0_ref[:, lanes] = grads[:rows]
        g2_ref[:, lanes] = grads[rows : 2 * rows].astype(bf16)
        g1_ref[:, lanes] = grads[2 * rows :].astype(bf16)
        return loss

    loss = lax.fori_loop(0, kv_count, one_group, entropy)
    loss_ref[...] = loss * (1.0 / heads)


def output_kernel(weight_ref, v0_ref, v1_ref, v2_ref, out_ref):
    bf16, f32 = jnp.bfloat16, jnp.float32
    rows = v0_ref.shape[0]
    group = weight_ref.shape[2] // rows
    for g in range(weight_ref.shape[0]):
        lanes = slice(g * HEAD_DIM, (g + 1) * HEAD_DIM)
        values = jnp.concatenate([v0_ref[:, lanes], v2_ref[:, lanes], v1_ref[:, lanes]], axis=0)
        flipped = jnp.dot(
            values.astype(f32).T.astype(bf16), weight_ref[g], preferred_element_type=f32
        )
        for i in range(group):
            h = g * group + i
            out_ref[:, h * HEAD_DIM : (h + 1) * HEAD_DIM] = (
                flipped[:, i * rows : (i + 1) * rows].T.astype(bf16)
            )


def attend(start, queries, keys, pick, prob):
    rows, kv_width = keys[0].shape
    kv_count = kv_width // HEAD_DIM
    group = queries.shape[1] // kv_width
    bf16, f32 = jnp.bfloat16, jnp.float32
    struct = jax.ShapeDtypeStruct
    return pl.pallas_call(
        attend_kernel,
        out_shape=[
            struct((rows, kv_width), f32),
            struct((rows, kv_width), bf16),
            struct((rows, kv_width), bf16),
            struct((1, rows), f32),
            struct((kv_count, (SPAN + 1) * rows, group * rows), bf16),
        ],
        in_specs=whole(7),
        out_specs=whole(5),
        scratch_shapes=[pltpu.VMEM(pick.shape[::-1], f32)] * 2,
        compiler_params=GRANT,
        name="attend",
    )(start.reshape(1, rows), queries, *keys, pick, prob)


def attend_output(weights, values):
    rows = values[0].shape[0]
    heads = weights.shape[0] * weights.shape[2] // rows
    return pl.pallas_call(
        output_kernel,
        out_shape=jax.ShapeDtypeStruct((rows, heads * HEAD_DIM), jnp.bfloat16),
        in_specs=whole(4),
        out_specs=whole()[0],
        compiler_params=GRANT,
        name="attend_output",
    )(weights, *values)


def whole(count=1):
    return [pl.BlockSpec(memory_space=pltpu.VMEM)] * count


def pack_rows(hidden, queries, values, row_target, seq_count):
    rows = hidden.shape[0]
    tiles = (hidden.shape[1] + queries.shape[1] + values.shape[1]) // HEAD_DIM
    main = tiles - tiles // 4
    return pl.pallas_call(
        pack_kernel,
        out_shape=jax.ShapeDtypeStruct((seq_count * 8, (main + 1) * HEAD_DIM), jnp.bfloat16),
        in_specs=whole(4),
        out_specs=whole()[0],
        compiler_params=GRANT,
        name="pack_rows",
    )(row_target.reshape(1, rows), hidden, queries, values)


def project(got, place_of, own_half, other_half, cosine, sine, sides):
    rows, (width, kv_width) = cosine.shape[0], own_half.shape
    struct = jax.ShapeDtypeStruct
    return pl.pallas_call(
        functools.partial(project_kernel, sides),
        out_shape=[struct((rows, w), jnp.bfloat16) for w in (kv_width, width, width)],
        in_specs=[pl.BlockSpec(memory_space=pltpu.SMEM)] + whole(5),
        out_specs=whole(3),
        scratch_shapes=[pltpu.VMEM((rows, width), jnp.bfloat16)] * 2,
        compiler_params=GRANT,
        name="project",
    )(place_of, got, own_half, other_half, cosine, sine)


def unpack_rest(got, rows, width, kv_width):
    return pl.pallas_call(
        rest_kernel,
        out_shape=[jax.ShapeDtypeStruct((rows, w), jnp.bfloat16) for w in (width, kv_width)],
        in_specs=whole(),
        out_specs=whole(2),
        compiler_params=GRANT,
        name="unpack_rest",
    )(got)


def step(
    hidden, queries, values, row_target, key_weight, dialogue_lengths, teacher_pick, teacher_prob
):
    bf16, f32 = jnp.bfloat16, jnp.float32
    local_rows, width = hidden.shape
    seq_count = lax.axis_size(SEQ)
    seq_index = lax.axis_index(SEQ)
    lines = lax.axis_size("y")
    device_count = seq_count * lines * lax.axis_size("core")
    kv_width = values.shape[1]

    place_of = jnp.stack([lax.axis_index("core"), lax.axis_index("y")]).astype(jnp.int32)

    plane_rows = exchange(jnp.broadcast_to(key_weight, (seq_count,) + key_weight.shape), SEQ)
    plane_rows = plane_rows.reshape(local_rows, kv_width)
    turned = [plane_rows]
    for by in range(1, lines):
        turned.append(line_shift(plane_rows, by))
    own_half = jnp.concatenate(turned, axis=0)
    other_half = core_swap(own_half)

    parcels = pack_rows(hidden, queries, values, row_target, seq_count)
    received = exchange(parcels.reshape(seq_count, 8, -1), SEQ)
    got = received.reshape(seq_count * 8, -1)
    positions = seq_index * local_rows + jnp.arange(local_rows, dtype=jnp.int32)
    cosine, sine = turn_angles(positions)
    keys_seq, mine, theirs = project(
        got,
        place_of,
        own_half,
        other_half,
        jnp.concatenate([cosine[:, 0], cosine[:, 0]], axis=1),
        jnp.concatenate([-sine[:, 0], sine[:, 0]], axis=1),
        lax.axis_size(ACROSS),
    )
    queries_seq, values_seq = unpack_rest(got, local_rows, width, kv_width)

    starts = dialogue_starts(dialogue_lengths[0], positions)
    near_keys = []
    for by in range(1, SPAN + 1):
        near_keys.append(seq_shift(keys_seq, by))
    own_grad, grad_1, grad_2, token_loss, weights = attend(
        starts - seq_index * local_rows,
        queries_seq,
        [keys_seq] + near_keys,
        teacher_pick,
        teacher_prob,
    )
    theirs, own_grad = lax.optimization_barrier((theirs, own_grad))
    partner = core_swap(theirs)
    rotated_grad = (
        own_grad + seq_shift(grad_1, -1).astype(f32) + seq_shift(grad_2, -2).astype(f32)
    )
    key_grad = rotate(rotated_grad, cosine, -sine).astype(bf16)

    inverse_root = (local_rows * device_count) ** (-0.5)

    def term(columns, grads):
        return jnp.einsum("td,tc->dc", columns, grads, preferred_element_type=f32)

    summed = (term(mine, key_grad) + term(partner, core_swap(key_grad))).astype(bf16)
    sides = lax.axis_size(ACROSS)
    pieces = jnp.transpose(summed.reshape(lines, sides, -1, kv_width), (1, 0, 2, 3))
    values_late, pieces = lax.optimization_barrier(
        (values_seq, pieces.reshape(sides, -1, kv_width))
    )
    line = jnp.sum(exchange(pieces, ACROSS).astype(f32), axis=0).astype(bf16)
    values_all = [values_seq]
    for by in range(1, SPAN + 1):
        values_all.append(seq_shift(values_late, by))
    attn_out = attend_output(weights, values_all)
    last = exchange(line.reshape(-1, 4, kv_width), ("y", "z"))
    weight_grad = jnp.sum(last.astype(f32), axis=0) * inverse_root
    return (attn_out, token_loss.reshape(local_rows), weight_grad)


def solution(mesh):
    fine = Mesh(np.asarray(mesh.devices).reshape(8, 2, 8, 2, 2), EVERY)
    pack = ("y", "core")
    placed = (
        P(EVERY, None),
        P(EVERY, None),
        P(EVERY, None),
        P(EVERY),
        P(EVERY, None),
        P(pack, None),
        P(EVERY, None),
        P(EVERY, None),
    )
    return jax.shard_map(
        step,
        mesh=fine,
        in_specs=placed,
        out_specs=(P(EVERY, None), P(EVERY), P(EVERY, None)),
        check_vma=False,
    )
```
